256 devices in a mesh: facet: 16 (over z_hi, x, core), col: 16 (over y, z_lo).
Axes of the slice: x: 4, y: 4, z: 8 (z_hi: 2, z_lo: 4; z = z_hi * 4 + z_lo), core: 2. Of those that a mesh axis runs over, the one named last changes fastest.
Arguments:
- facet_spectra: bfloat16 [2, 16, 2, 512, 16384], P(None, 'facet', None, None, 'col'), may hold values from -6 to 6
- facet_offsets: int32 [16, 2], P('facet'), may hold values from 0 to 65535
- column_index: int32 [2], replicated, may hold values from 0 to 145
- subgrid_offsets: int32 [2, 16], P(None, 'col'), may hold values from 0 to 65532, as said below
- weights: bfloat16 [2, 16, 512, 512], P(None, 'col', 'facet'), may hold values from 0.25 to 4
Outputs:
- subgrids: bfloat16 [2, 16, 2, 512, 512], P(None, 'col', None, 'facet')
- facet_updates: bfloat16 [2, 16, 2, 512, 16384], P(None, 'facet', None, None, 'col')
The draws below stay inside these ranges and needn't reach their ends.
Inputs may be any that keep to these rules, and one draw needn't show every extreme that they name: `subgrid_offsets`: every offset is a multiple of 4; subgrid s of a column has position p = offset / 4 with (s // 1) * 1024 <= p < (s + 1) * 1024. In every column some subgrid has p exactly at such a lower end, and some subgrid has p at (s + 1) * 1024 - 128 // 2 + 1 or above.
All inputs are finite; a program needn't handle non-finite values.
Results may differ from the reference program's by a relative error of at most 0.015.
Values may be sent and summed in bfloat16 or wider, within the bound.
A program may use at most 64 MiB of HBM per device.

```python
import math
import jax
import jax.numpy as jnp
from jax import lax

IMAGE = 65536
XM = 512
WM = 128
YP_DEV = 1024
YP = 16384
XA = 448
COLS = 2
SUB_DEV = 1
SUBS = 16
FACETS = 16
N_FACET = 16
N_COL = 16


def draw_subgrid_offsets(key, part):
    half = WM // 2
    span = YP_DEV // SUB_DEV
    key_inner, key_first, key_last, key_variety, key_pick, key_opposite = jax.random.split(key, 6)
    slots = jnp.arange(SUB_DEV, dtype=jnp.int32)[None, None, :]
    shards = jnp.arange(N_COL, dtype=jnp.int32)[None, :, None]
    inner = slots * span + jax.random.randint(key_inner, (COLS, N_COL, SUB_DEV), 0, span)
    first = jax.random.randint(key_first, (COLS, N_COL, SUB_DEV), 0, half)
    last = YP_DEV - half + 1 + jax.random.randint(key_last, (COLS, N_COL, SUB_DEV), 0, half - 1)
    variety = jax.random.randint(key_variety, (COLS, N_COL, SUB_DEV), 0, 3)
    places = jnp.where(variety == 0, first, jnp.where(variety == 1, last, inner))
    chosen = jax.random.randint(key_pick, (COLS, 1, 1), 0, N_COL)
    opposite = (chosen + 1 + jax.random.randint(key_opposite, (COLS, 1, 1), 0, N_COL - 1)) % N_COL
    places = jnp.where((shards == chosen) & (slots == 0), 0, places)
    places = jnp.where((shards == opposite) & (slots == SUB_DEV - 1), last, places)
    centres = places + shards * YP_DEV
    return (centres * (IMAGE // (YP_DEV * N_COL))).reshape(COLS, SUB_DEV * N_COL).astype(jnp.int32)


def place_ends(entries, stream_key, low, high):
    longest = entries.shape.index(max(entries.shape))
    spots = []
    for shift in (0, 1):
        where = [jax.random.randint(jax.random.fold_in(stream_key, axis), (), 0, length) for axis, length in enumerate(entries.shape)]
        where[longest] = (where[longest] + shift) % entries.shape[longest]
        spots.append(tuple(where))
    return entries.at[spots[0]].set(low).at[spots[1]].set(high)


def levels(key, extent, cuts, least, largest):
    loudness, own = 1.0, jax.random.fold_in(key, 6)
    for position, blocks in cuts:
        steps = jnp.exp(jax.random.uniform(jax.random.fold_in(own, position), (blocks,), jnp.float32, least / len(cuts), largest / len(cuts)))
        loudness = loudness * jnp.repeat(steps, extent[position] // blocks).reshape([-1 if axis == position else 1 for axis in range(len(extent))])
    return loudness


def noise(own_key, extent, deviation, limit, cuts=(), kind=jnp.bfloat16):
    entries = deviation * jax.random.normal(own_key, extent, jnp.float32)
    if cuts:
        entries = entries * levels(own_key, extent, cuts, -0.22, 0.18)
    return jnp.clip(entries, -limit, limit).astype(kind)


def setup_inputs(seed: int = 0) -> dict:
    arg_keys = jax.random.split(jax.random.key(seed), 6)
    return {
        "facet_spectra": noise(arg_keys[0], (COLS, FACETS, 2, XM, YP), 1.0, 6.0, ((1, 16), (4, 16))),
        "facet_offsets": place_ends(jax.random.randint(arg_keys[1], (FACETS, 2), 0, IMAGE), jax.random.fold_in(arg_keys[1], 1), 0, IMAGE - 1).astype(jnp.int32),
        "column_index": jax.random.randint(arg_keys[2], (COLS,), 0, IMAGE // XA).astype(jnp.int32),
        "subgrid_offsets": draw_subgrid_offsets(jax.random.fold_in(arg_keys[5], 71), 0),
        "weights": jnp.clip(jnp.exp(math.log(4.0) - 2.7725887 * jax.random.uniform(arg_keys[4], (COLS, SUBS, XM, XM), jnp.float32) ** levels(arg_keys[4], (COLS, SUBS, XM, XM), ((1, 16), (2, 16)), -0.2, 0.2)), 0.25, 4.0).astype(jnp.bfloat16),
    }


TAU = 2.0 * math.pi

def modular(first, second, image):
    upper = second // 256
    lower = second % 256
    return (first * upper % (image // 256) * 256 + first * lower) % image

def make_table(facets):
    place = jnp.arange(WM, dtype=jnp.int32)
    cell = jnp.arange(XM, dtype=jnp.int32)
    turns = (place[:, None] - WM // 2) * (cell[None, :] - XM // 2) % XM
    angle = TAU * turns.astype(jnp.float32) / XM
    relative = (place.astype(jnp.float32) + 0.5 - WM / 2.0) / (WM / 2.0)
    taper = (0.3 + 0.7 * (1.0 - relative * relative)) / jnp.sqrt(jnp.float32(WM * facets))
    return ((taper[:, None] * jnp.cos(angle)).astype(jnp.bfloat16), (taper[:, None] * jnp.sin(angle)).astype(jnp.bfloat16))

def phases(column_pos, offsets, indices):
    first = modular(column_pos, offsets[0], IMAGE)
    second = indices * offsets[1] % YP
    return TAU * (first.astype(jnp.float32) / IMAGE + second.astype(jnp.float32) / YP)

def mult(form, left, right):
    return jnp.einsum(form, left.astype(jnp.float32), right.astype(jnp.float32), precision=lax.Precision.HIGHEST)

def reference(facet_spectra, facet_offsets, column_index, subgrid_offsets, weights):
    real_tab, imag_tab = make_table(N_FACET)
    grids = []
    updates = []
    for column in range(COLS):
        centres = subgrid_offsets[column] // (IMAGE // YP)
        indices = ((centres[:, None] - WM // 2 + jnp.arange(WM, dtype=jnp.int32)[None, :]) % YP).astype(jnp.int32)
        column_pos = column_index[column] * XA

        def add_facet(total, items):
            spectrum, offsets = items
            angle = phases(column_pos, offsets, indices)
            cosine = jnp.cos(angle)
            sine = jnp.sin(angle)
            window = spectrum[:, :, indices].astype(jnp.float32)
            real_part = (window[0] * cosine + window[1] * sine).astype(jnp.bfloat16)
            imag_part = (window[1] * cosine - window[0] * sine).astype(jnp.bfloat16)
            return (total + jnp.stack([real_part, imag_part]).astype(jnp.float32), None)
        start = jnp.zeros((2, XM, SUBS, WM), jnp.float32)
        summed, _ = lax.scan(add_facet, start, (facet_spectra[column], facet_offsets))
        grid_real = mult('xsm,ml->sxl', summed[0], real_tab) - mult('xsm,ml->sxl', summed[1], imag_tab)
        grid_imag = mult('xsm,ml->sxl', summed[0], imag_tab) + mult('xsm,ml->sxl', summed[1], real_tab)
        grid = jnp.stack([grid_real, grid_imag], axis=1).astype(jnp.bfloat16)
        grids.append(grid)
        scaled = (grid.astype(jnp.float32) * weights[column].astype(jnp.float32)[:, None]).astype(jnp.bfloat16)
        back_real = mult('sxl,ml->sxm', scaled[:, 0], real_tab) + mult('sxl,ml->sxm', scaled[:, 1], imag_tab)
        back_imag = mult('sxl,ml->sxm', scaled[:, 1], real_tab) - mult('sxl,ml->sxm', scaled[:, 0], imag_tab)

        def spread(offsets):
            angle = phases(column_pos, offsets, indices)
            cosine = jnp.cos(angle)[:, None, :]
            sine = jnp.sin(angle)[:, None, :]
            upd_real = back_real * cosine - back_imag * sine
            upd_imag = back_imag * cosine + back_real * sine
            pieces = jnp.stack([upd_real, upd_imag]).transpose(0, 2, 1, 3)
            target = jnp.zeros((2, XM, YP), jnp.float32)
            return target.at[:, :, indices].add(pieces).astype(jnp.bfloat16)
        updates.append(lax.map(spread, facet_offsets))
    return (jnp.stack(grids), jnp.stack(updates))
```

```python
import math

import jax
import jax.numpy as jnp
import numpy as np
from jax import lax
from jax.experimental import pallas as pl
from jax.experimental.pallas import tpu as pltpu
from jax.sharding import PartitionSpec as P

XM = 512
WM = 128
XA = 448
SHARD = 1024
HALF = WM // 2
FACETS = 16
F32 = jnp.float32
BF16 = jnp.bfloat16
I32 = jnp.int32
MESH = pl.DeviceIdType.MESH


def tables():
    place = np.arange(WM)
    cell = np.arange(XM)
    turns = (place[:, None] - WM // 2) * (cell[None, :] - XM // 2) % XM
    angle = 2.0 * math.pi * turns / XM
    relative = (place + 0.5 - WM / 2.0) / (WM / 2.0)
    taper = (0.3 + 0.7 * (1.0 - relative * relative)) / math.sqrt(WM * FACETS)
    real = (taper[:, None] * np.cos(angle)).astype(np.float32)
    imag = (taper[:, None] * np.sin(angle)).astype(np.float32)
    full = np.block([[real, imag], [-imag, real]])
    return full.astype(BF16), np.ascontiguousarray(full.T).astype(BF16)


def phase(turn):
    quarter = lax.shift_right_logical(turn + 8192, 14)
    angle = (turn - quarter * 16384).astype(F32) * (2.0 * math.pi / 65536.0)
    square = angle * angle
    sine = angle * (
        1.0 + square * (-1.0 / 6.0 + square * (1.0 / 120.0 + square * (-1.0 / 5040.0 + square * (1.0 / 362880.0))))
    )
    cosine = 1.0 + square * (-0.5 + square * (1.0 / 24.0 + square * (-1.0 / 720.0 + square * (1.0 / 40320.0))))
    odd = (quarter & 1) == 1
    first = jnp.where(odd, sine, cosine)
    second = jnp.where(odd, cosine, sine)
    cosine = jnp.where(((quarter + 1) & 2) == 2, -first, first)
    sine = jnp.where((quarter & 2) == 2, -second, second)
    return cosine, sine


def turns(column_pos, first, second, k):
    return (column_pos * first + 4 * (k * second)) & 65535


def iota(shape, dim):
    return lax.broadcasted_iota(I32, shape, dim)


def dot(a, b):
    return jnp.dot(a, b, preferred_element_type=F32)


def exchange_kernel(
    offs_ref, colidx_ref, sub_ref, x_hbm, w_hbm, t_hbm, tt_hbm,
    grid_out, u_out,
    x_v, w_v, t_v, tt_v, y, r1, r2a, r2b, rl, rr, s2, r3, above, below, eo, g,
    grid_v, local_sem, ss, rs,
):
    f = lax.axis_index("facet")
    c = lax.axis_index("col")
    core = f % 2
    x = (f // 2) % 4
    zh = f // 8
    left = (x + 3) % 4
    right = (x + 1) % 4
    far = (x + 2) % 4
    f_core = f + 1 - 2 * core
    f_left = zh * 8 + left * 2 + core
    f_right = zh * 8 + right * 2 + core
    f_z = (f + 8) % 16
    c_prev = (c + 15) % 16
    c_next = (c + 1) % 16

    barrier = pltpu.get_barrier_semaphore()
    peers = [
        (f_core, c), (f_left, c), (f_right, c), (f_z, c),
        (f, c_prev), (f_z, c_prev), (f, c_next), (f_z, c_next),
    ]
    for peer in peers:
        pl.semaphore_signal(barrier, inc=1, device_id=peer, device_id_type=MESH)

    loads = [
        pltpu.make_async_copy(x_hbm.at[0], x_v.at[0], local_sem.at[0]),
        pltpu.make_async_copy(x_hbm.at[1], x_v.at[1], local_sem.at[1]),
        pltpu.make_async_copy(t_hbm, t_v, local_sem.at[2]),
        pltpu.make_async_copy(tt_hbm, tt_v, local_sem.at[3]),
        pltpu.make_async_copy(w_hbm, w_v, local_sem.at[4]),
    ]
    for load in loads:
        load.start()

    sends = []

    def send(src, dst, f_to, c_to=None):
        index = len(sends)
        copy = pltpu.make_async_remote_copy(
            src_ref=src, dst_ref=dst, send_sem=ss.at[index], recv_sem=rs.at[index],
            device_id=(f_to, c if c_to is None else c_to), device_id_type=MESH,
        )
        copy.start()
        sends.append(copy)
        return copy

    lane = iota((16, 128), 1)
    starts = []

    def phased(col):
        position = lax.shift_right_arithmetic(sub_ref[col, 0], 2)
        start = position - c * SHARD - HALF
        starts.append(start)
        column_pos = colidx_ref[col] * XA
        first, second = offs_ref[0, 0], offs_ref[0, 1]
        cosine, sine = phase(turns(column_pos, first, second, c * SHARD + start + iota((8, 128), 1)))
        cosine, sine = cosine[0:1], sine[0:1]
        spot = iota((8, 128), 1)
        spot = c * SHARD + jnp.where(spot < HALF, spot, SHARD - 128 + spot)
        cosine_e, sine_e = phase(turns(column_pos, first, second, spot))
        cosine_e, sine_e = cosine_e[0:1], sine_e[0:1]
        pick = (iota((SHARD, 128), 0) == iota((SHARD, 128), 1) + start).astype(F32).astype(BF16)
        wide = iota((128, 128), 1) < HALF

        def rows(q, carry):
            span = pl.ds(pl.multiple_of(q * 128, 128), 128)
            main_re = dot(x_v[col, 0, span], pick)
            main_im = dot(x_v[col, 1, span], pick)
            out_re = (main_re * cosine + main_im * sine).astype(BF16)
            out_im = (main_im * cosine - main_re * sine).astype(BF16)
            edge_re = jnp.where(wide, x_v[col, 0, span, 0:128].astype(F32), x_v[col, 0, span, SHARD - 128:SHARD].astype(F32))
            edge_im = jnp.where(wide, x_v[col, 1, span, 0:128].astype(F32), x_v[col, 1, span, SHARD - 128:SHARD].astype(F32))
            e_re = edge_re * cosine_e + edge_im * sine_e
            e_im = edge_im * cosine_e - edge_re * sine_e
            swap_re = pltpu.roll(e_re, 64, 1)
            swap_im = pltpu.roll(e_im, 64, 1)
            for j in range(4):
                xx, cc = (q % 2) * 2 + j // 2, j % 2
                block = y.at[col, cc, xx, q // 2]
                a, b, d = 32 * j, 32 * j + 16, 32 * j + 32
                block[0:32] = out_re[a:d]
                block[32:64] = out_im[a:d]
                block[64:80] = jnp.where(lane < HALF, e_re[a:b], swap_re[b:d]).astype(BF16)
                block[80:96] = jnp.where(lane < HALF, e_im[a:b], swap_im[b:d]).astype(BF16)
                block[96:112] = jnp.where(lane < HALF, swap_re[a:b], e_re[b:d]).astype(BF16)
                block[112:128] = jnp.where(lane < HALF, swap_im[a:b], e_im[b:d]).astype(BF16)
            return carry

        lax.fori_loop(0, 4, rows, 0)

    order = [far, right, left, x]
    stage1 = []
    for col in range(2):
        loads[col].wait()
        phased(col)
        if col == 0:
            pl.semaphore_wait(barrier, len(peers))
        stage1.append([send(y.at[col, 1 - core, xx], r1.at[col, xx], f_core) for xx in order])

    def add(dst, *others):
        total = dst[...].astype(F32)
        for other in others:
            total = total + other[...].astype(F32)
        return total

    far_sent, near_sent = [], []
    for col in range(2):
        mine = y.at[col, core]
        stage1[col][0].wait_recv()
        mine[far] = add(mine.at[far], r1.at[col, far]).astype(BF16)
        far_sent.append((
            send(mine.at[far, 0], r2a.at[col], f_right),
            send(mine.at[far, 1], r2b.at[col], f_left),
        ))
        stage1[col][1].wait_recv()
        mine[right] = add(mine.at[right], r1.at[col, right]).astype(BF16)
        stage1[col][2].wait_recv()
        to_right = send(mine.at[right, 1], rl.at[col, 1], f_right)
        mine[left] = add(mine.at[left], r1.at[col, left]).astype(BF16)
        to_left = send(mine.at[left, 0], rr.at[col, 0], f_left)
        near_sent.append([to_right, to_left])

    for col in range(2):
        mine = y.at[col, core]
        far_sent[col][0].wait_recv()
        mine[right, 0] = add(mine.at[right, 0], r2a.at[col]).astype(BF16)
        near_sent[col].append(send(mine.at[right, 0], rl.at[col, 0], f_right))
        far_sent[col][1].wait_recv()
        mine[left, 1] = add(mine.at[left, 1], r2b.at[col]).astype(BF16)
        near_sent[col].append(send(mine.at[left, 1], rr.at[col, 1], f_left))
        stage1[col][3].wait_recv()

    stage3 = []
    other = 1 - zh
    for col in range(2):
        for copy in near_sent[col]:
            copy.wait_recv()
        mine = y.at[col, core, x]
        for zz in (other, zh):
            s2[col, zz] = add(mine.at[zz], r1.at[col, x, zz], rl.at[col, zz], rr.at[col, zz]).astype(BF16)
        copies = [send(s2.at[col, other, pl.ds(0, 64)], r3.at[col], f_z)]
        for k, (zz, f_to) in enumerate(((zh, f), (other, f_z))):
            copies.append(send(s2.at[col, zz, pl.ds(64, 32)], above.at[col, k], f_to, c_prev))
            copies.append(send(s2.at[col, zz, pl.ds(96, 32)], below.at[col, k], f_to, c_next))
        stage3.append(copies)

    for load in loads[2:]:
        load.wait()

    stage5 = []
    for col in range(2):
        start = starts[col]
        side0, side1 = iota((256, 256), 0), iota((256, 256), 1)

        def matrix(source, window):
            cell = (source & 63) + jnp.where(source < 128, -HALF, SHARD) - start
            same = (lax.shift_right_logical(source, 6) & 1) == lax.shift_right_logical(window, 7)
            return jnp.where(same & (cell == (window & 127)), 1.0, 0.0).astype(BF16)

        gather_in = matrix(side0, side1)
        gather_out = matrix(side1, side0)
        for copy in stage3[col]:
            copy.wait_recv()
        main = add(s2.at[col, zh, pl.ds(0, 64)], r3.at[col])
        low = add(below.at[col, 0], below.at[col, 1])
        high = add(above.at[col, 0], above.at[col, 1])
        edge = dot(jnp.concatenate([low, high], axis=1).astype(BF16), gather_in)
        edge_re = jnp.concatenate([edge[0:16, 0:128], edge[0:16, 128:256]], axis=0)
        edge_im = jnp.concatenate([edge[16:32, 0:128], edge[16:32, 128:256]], axis=0)
        window = jnp.concatenate([main[0:32] + edge_re, main[32:64] + edge_im], axis=1).astype(BF16)
        cells = dot(window, t_v[...]).astype(BF16)
        grid_v[col, 0] = cells[:, 0:XM]
        grid_v[col, 1] = cells[:, XM:2 * XM]
        weight = w_v[col].astype(F32)
        weight = jnp.concatenate([weight, weight], axis=1)
        scaled = (cells.astype(F32) * weight).astype(BF16)
        back = dot(scaled, tt_v[...]).astype(BF16)
        block = g.at[col, zh, x, core]
        block[0:32] = back[:, 0:128]
        block[32:64] = back[:, 128:256]
        packed = jnp.concatenate([
            jnp.concatenate([back[0:16, 0:128], back[16:32, 0:128]], axis=1),
            jnp.concatenate([back[0:16, 128:256], back[16:32, 128:256]], axis=1),
        ], axis=0)
        out_edge = dot(packed, gather_out).astype(BF16)
        eo[col, 0] = out_edge[:, 0:128]
        eo[col, 1] = out_edge[:, 128:256]
        home = g.at[col, zh, x, core]
        copies = [send(home.at[pl.ds(0, 64)], home.at[pl.ds(0, 64)], f_z)]
        for f_to in (f, f_z):
            copies.append(send(eo.at[col, 0], home.at[pl.ds(96, 32)], f_to, c_prev))
            copies.append(send(eo.at[col, 1], home.at[pl.ds(64, 32)], f_to, c_next))
        stage5.append(copies)

    grid_copy = pltpu.make_async_copy(grid_v, grid_out, local_sem.at[5])
    grid_copy.start()

    stage6 = []
    for col in range(2):
        for copy in stage5[col]:
            copy.wait_recv()
        block = g.at[col, :, x, core]
        stage6.append([send(block, block, f_right), send(block, block, f_left), send(block, block, f_core)])

    stage7, to_core = [], []
    for col in range(2):
        stage6[col][0].wait_recv()
        block = g.at[col, 0, left, core]
        onward = [send(block, block, f_right)]
        block = g.at[col, :, left, core]
        to_core.append([stage6[col][2], send(block, block, f_core)])
        stage6[col][1].wait_recv()
        block = g.at[col, 1, right, core]
        onward.append(send(block, block, f_left))
        block = g.at[col, :, right, core]
        to_core[col].append(send(block, block, f_core))
        stage7.append(onward)

    outs = []
    for col in range(2):
        for copy in stage7[col]:
            copy.wait_recv()
        block = g.at[col, :, far, core]
        to_core[col].append(send(block, block, f_core))
        for copy in to_core[col]:
            copy.wait_recv()
        out = pltpu.make_async_copy(g.at[col], u_out.at[col], local_sem.at[6 + col])
        out.start()
        outs.append(out)

    for copy in sends:
        copy.wait_send()
    grid_copy.wait()
    for out in outs:
        out.wait()


N_SENDS = 8 + 4 + 4 + 4 + 10 + 10 + 6 + 8 + 2


def exchange(offsets, column_index, subgrid_offsets, spectra, weights):
    table, table_t = tables()
    any_space = pl.BlockSpec(memory_space=pl.ANY)
    hbm = pl.BlockSpec(memory_space=pltpu.HBM)
    smem = pl.BlockSpec(memory_space=pltpu.SMEM)
    return pl.pallas_call(
        exchange_kernel,
        out_shape=(
            jax.ShapeDtypeStruct((2, 2, 32, XM), BF16),
            jax.ShapeDtypeStruct((2, 2, 4, 2, 128, 128), BF16),
        ),
        in_specs=[smem, smem, smem, hbm, hbm, hbm, hbm],
        out_specs=(any_space, any_space),
        scratch_shapes=[
            pltpu.VMEM((2, 2, XM, SHARD), BF16),
            pltpu.VMEM((2, 32, XM), BF16),
            pltpu.VMEM((256, 1024), BF16),
            pltpu.VMEM((1024, 256), BF16),
            pltpu.VMEM((2, 2, 4, 2, 128, 128), BF16),
            pltpu.VMEM((2, 4, 2, 128, 128), BF16),
            pltpu.VMEM((2, 128, 128), BF16),
            pltpu.VMEM((2, 128, 128), BF16),
            pltpu.VMEM((2, 2, 128, 128), BF16),
            pltpu.VMEM((2, 2, 128, 128), BF16),
            pltpu.VMEM((2, 2, 128, 128), BF16),
            pltpu.VMEM((2, 64, 128), BF16),
            pltpu.VMEM((2, 2, 32, 128), BF16),
            pltpu.VMEM((2, 2, 32, 128), BF16),
            pltpu.VMEM((2, 2, 32, 128), BF16),
            pltpu.VMEM((2, 2, 4, 2, 128, 128), BF16),
            pltpu.VMEM((2, 2, 32, XM), BF16),
            pltpu.SemaphoreType.DMA((8,)),
            pltpu.SemaphoreType.DMA((N_SENDS,)),
            pltpu.SemaphoreType.DMA((N_SENDS,)),
        ],
        compiler_params=pltpu.CompilerParams(
            collective_id=0, has_side_effects=True, vmem_limit_bytes=40 << 20
        ),
        name="exchange",
    )(offsets, column_index, subgrid_offsets, spectra, weights, jnp.asarray(table), jnp.asarray(table_t))


def place_kernel(offs_ref, colidx_ref, sub_ref, here_ref, u_ref, grid_ref, out_ref, grid_out):
    col = pl.program_id(0)
    c = here_ref[0]
    grid_out[...] = grid_ref[...]
    out_ref[...] = jnp.zeros_like(out_ref)
    position = lax.shift_right_arithmetic(sub_ref[col, 0], 2)
    start = position - c * SHARD - HALF
    base = jnp.clip(lax.shift_right_arithmetic(start, 7), 0, SHARD // 128 - 2) * 128
    column_pos = colidx_ref[col] * XA
    first, second = offs_ref[0, 0], offs_ref[0, 1]
    cosine, sine = phase(turns(column_pos, first, second, c * SHARD + base + iota((8, 256), 1)))
    cosine, sine = cosine[0:1], sine[0:1]
    spot = iota((8, 128), 1)
    spot = c * SHARD + jnp.where(spot < HALF, spot, SHARD - 128 + spot)
    cosine_e, sine_e = phase(turns(column_pos, first, second, spot))
    cosine_e, sine_e = cosine_e[0:1], sine_e[0:1]
    put = (iota((128, 256), 1) + base == iota((128, 256), 0) + start).astype(F32).astype(BF16)
    lane = iota((16, 128), 1)
    wide = iota((32, 128), 1) < HALF
    blocks = u_ref.shape[2]
    tiles = pl.ds(pl.multiple_of(base, 128), 256)
    for xx in range(blocks):
        for cc in range(2):
            block = u_ref.at[0, 0, xx, cc]
            rows = pl.ds((xx * 2 + cc) * 32, 32)
            low_re, low_im = block[64:80].astype(F32), block[80:96].astype(F32)
            top_re, top_im = block[96:112].astype(F32), block[112:128].astype(F32)
            edges = []
            for low, top in ((low_re, top_re), (low_im, top_im)):
                edges.append(jnp.concatenate([
                    jnp.where(lane < HALF, low, pltpu.roll(top, 64, 1)),
                    jnp.where(lane < HALF, pltpu.roll(low, 64, 1), top),
                ], axis=0))
            edge_re = edges[0] * cosine_e - edges[1] * sine_e
            edge_im = edges[1] * cosine_e + edges[0] * sine_e
            zero = jnp.zeros_like(edge_re)
            for part, edge in ((0, edge_re), (1, edge_im)):
                out_ref[0, part, rows, 0:128] = jnp.where(wide, edge, zero).astype(BF16)
                out_ref[0, part, rows, SHARD - 128:SHARD] = jnp.where(wide, zero, edge).astype(BF16)
            moved = dot(block[0:64], put)
            main_re, main_im = moved[0:32], moved[32:64]
            out_re = main_re * cosine - main_im * sine
            out_im = main_im * cosine + main_re * sine
            for part, value in ((0, out_re), (1, out_im)):
                out_ref[0, part, rows, tiles] = (out_ref[0, part, rows, tiles].astype(F32) + value).astype(BF16)


def place(offsets, column_index, subgrid_offsets, here, gathered, grids):
    smem = pl.BlockSpec(memory_space=pltpu.SMEM)
    return pl.pallas_call(
        place_kernel,
        grid=(2, 2),
        out_shape=(
            jax.ShapeDtypeStruct((2, 2, XM, SHARD), BF16),
            jax.ShapeDtypeStruct((2, 2, 32, XM), BF16),
        ),
        in_specs=[
            smem, smem, smem, smem,
            pl.BlockSpec((1, 1, 4, 2, 128, 128), lambda i, j: (i, j, 0, 0, 0, 0)),
            pl.BlockSpec((1, 2, 32, XM), lambda i, j: (i, 0, 0, 0)),
        ],
        out_specs=(
            pl.BlockSpec((1, 2, XM // 2, SHARD), lambda i, j: (i, 0, j, 0)),
            pl.BlockSpec((1, 2, 32, XM), lambda i, j: (i, 0, 0, 0)),
        ),
        compiler_params=pltpu.CompilerParams(dimension_semantics=("arbitrary", "arbitrary")),
        name="place",
    )(offsets, column_index, subgrid_offsets, here, gathered, grids)


def per_device(facet_spectra, facet_offsets, column_index, subgrid_offsets, weights):
    spectra = facet_spectra.reshape(2, 2, XM, SHARD)
    grids, gathered = exchange(
        facet_offsets, column_index, subgrid_offsets, spectra, weights.reshape(2, 32, XM)
    )
    here = lax.axis_index("col").astype(I32).reshape(1)
    updates, grids = place(facet_offsets, column_index, subgrid_offsets, here, gathered, grids)
    return grids.reshape(2, 1, 2, 32, XM), updates.reshape(2, 1, 2, XM, SHARD)


def solution(mesh):
    in_specs = (
        P(None, "facet", None, None, "col"),
        P("facet", None),
        P(),
        P(None, "col"),
        P(None, "col", "facet", None),
    )
    out_specs = (P(None, "col", None, "facet", None), P(None, "facet", None, None, "col"))
    return jax.shard_map(
        per_device, mesh=mesh, in_specs=in_specs, out_specs=out_specs, check_vma=False
    )
```

```python
import math

import jax
import jax.numpy as jnp
import numpy as np
from jax import lax
from jax.experimental import pallas as pl
from jax.experimental.pallas import tpu as pltpu
from jax.sharding import PartitionSpec as P

XM = 512
WM = 128
XA = 448
SHARD = 1024
HALF = WM // 2
FACETS = 16
F32 = jnp.float32
BF16 = jnp.bfloat16
I32 = jnp.int32
MESH = pl.DeviceIdType.MESH


def tables():
    place = np.arange(WM)
    cell = np.arange(XM)
    turns = (place[:, None] - WM // 2) * (cell[None, :] - XM // 2) % XM
    angle = 2.0 * math.pi * turns / XM
    relative = (place + 0.5 - WM / 2.0) / (WM / 2.0)
    taper = (0.3 + 0.7 * (1.0 - relative * relative)) / math.sqrt(WM * FACETS)
    real = (taper[:, None] * np.cos(angle)).astype(np.float32)
    imag = (taper[:, None] * np.sin(angle)).astype(np.float32)
    full = np.block([[real, imag], [-imag, real]])
    return full.astype(BF16), np.ascontiguousarray(full.T).astype(BF16)


def phase(turn):
    quarter = lax.shift_right_logical(turn + 8192, 14)
    angle = (turn - quarter * 16384).astype(F32) * (2.0 * math.pi / 65536.0)
    square = angle * angle
    sine = angle * (
        1.0 + square * (-1.0 / 6.0 + square * (1.0 / 120.0 + square * (-1.0 / 5040.0 + square * (1.0 / 362880.0))))
    )
    cosine = 1.0 + square * (-0.5 + square * (1.0 / 24.0 + square * (-1.0 / 720.0 + square * (1.0 / 40320.0))))
    odd = (quarter & 1) == 1
    first = jnp.where(odd, sine, cosine)
    second = jnp.where(odd, cosine, sine)
    cosine = jnp.where(((quarter + 1) & 2) == 2, -first, first)
    sine = jnp.where((quarter & 2) == 2, -second, second)
    return cosine, sine


def turns(column_pos, first, second, k):
    return (column_pos * first + 4 * (k * second)) & 65535


def iota(shape, dim):
    return lax.broadcasted_iota(I32, shape, dim)


def dot(a, b):
    return jnp.dot(a, b, preferred_element_type=F32)


def exchange_kernel(
    offs_ref, colidx_ref, sub_ref, x_hbm, w_hbm, t_hbm, tt_hbm,
    grid_out, u_out,
    x_v, w_v, t_v, tt_v, y, r1, r2a, r2b, rl, rr, s2, r3, above, below, eo, g,
    grid_v, local_sem, ss, rs,
):
    f = lax.axis_index("facet")
    c = lax.axis_index("col")
    core = f % 2
    x = (f // 2) % 4
    zh = f // 8
    left = (x + 3) % 4
    right = (x + 1) % 4
    far = (x + 2) % 4
    f_core = f + 1 - 2 * core
    f_left = zh * 8 + left * 2 + core
    f_right = zh * 8 + right * 2 + core
    f_z = (f + 8) % 16
    c_prev = (c + 15) % 16
    c_next = (c + 1) % 16

    barrier = pltpu.get_barrier_semaphore()
    peers = [
        (f_core, c), (f_left, c), (f_right, c), (f_z, c),
        (f, c_prev), (f_z, c_prev), (f, c_next), (f_z, c_next),
    ]
    for peer in peers:
        pl.semaphore_signal(barrier, inc=1, device_id=peer, device_id_type=MESH)

    loads = [
        pltpu.make_async_copy(x_hbm.at[0], x_v.at[0], local_sem.at[0]),
        pltpu.make_async_copy(x_hbm.at[1], x_v.at[1], local_sem.at[1]),
        pltpu.make_async_copy(t_hbm, t_v, local_sem.at[2]),
        pltpu.make_async_copy(tt_hbm, tt_v, local_sem.at[3]),
        pltpu.make_async_copy(w_hbm, w_v, local_sem.at[4]),
    ]
    for load in loads:
        load.start()

    sends = []

    def send(src, dst, f_to, c_to=None):
        index = len(sends)
        copy = pltpu.make_async_remote_copy(
            src_ref=src, dst_ref=dst, send_sem=ss.at[index], recv_sem=rs.at[index],
            device_id=(f_to, c if c_to is None else c_to), device_id_type=MESH,
        )
        copy.start()
        sends.append(copy)
        return copy

    lane = iota((16, 128), 1)
    starts = []

    def phased(col):
        position = lax.shift_right_arithmetic(sub_ref[col], 2)
        start = position - c * SHARD - HALF
        starts.append(start)
        column_pos = colidx_ref[col] * XA
        first, second = offs_ref[0, 0], offs_ref[0, 1]
        cosine, sine = phase(turns(column_pos, first, second, c * SHARD + start + iota((8, 128), 1)))
        cosine, sine = cosine[0:1], sine[0:1]
        spot = iota((8, 128), 1)
        spot = c * SHARD + jnp.where(spot < HALF, spot, SHARD - 128 + spot)
        cosine_e, sine_e = phase(turns(column_pos, first, second, spot))
        cosine_e, sine_e = cosine_e[0:1], sine_e[0:1]
        pick = (iota((SHARD, 128), 0) == iota((SHARD, 128), 1) + start).astype(F32).astype(BF16)
        wide = iota((128, 128), 1) < HALF

        def rows(q, carry):
            span = pl.ds(pl.multiple_of(q * 128, 128), 128)
            main_re = dot(x_v[col, 0, span], pick)
            main_im = dot(x_v[col, 1, span], pick)
            out_re = (main_re * cosine + main_im * sine).astype(BF16)
            out_im = (main_im * cosine - main_re * sine).astype(BF16)
            edge_re = jnp.where(wide, x_v[col, 0, span, 0:128].astype(F32), x_v[col, 0, span, SHARD - 128:SHARD].astype(F32))
            edge_im = jnp.where(wide, x_v[col, 1, span, 0:128].astype(F32), x_v[col, 1, span, SHARD - 128:SHARD].astype(F32))
            e_re = edge_re * cosine_e + edge_im * sine_e
            e_im = edge_im * cosine_e - edge_re * sine_e
            swap_re = pltpu.roll(e_re, 64, 1)
            swap_im = pltpu.roll(e_im, 64, 1)
            for j in range(4):
                xx, cc = (q % 2) * 2 + j // 2, j % 2
                block = y.at[col, cc, xx, q // 2]
                a, b, d = 32 * j, 32 * j + 16, 32 * j + 32
                block[0:32] = out_re[a:d]
                block[32:64] = out_im[a:d]
                block[64:80] = jnp.where(lane < HALF, e_re[a:b], swap_re[b:d]).astype(BF16)
                block[80:96] = jnp.where(lane < HALF, e_im[a:b], swap_im[b:d]).astype(BF16)
                block[96:112] = jnp.where(lane < HALF, swap_re[a:b], e_re[b:d]).astype(BF16)
                block[112:128] = jnp.where(lane < HALF, swap_im[a:b], e_im[b:d]).astype(BF16)
            return carry

        lax.fori_loop(0, 4, rows, 0)

    order = [far, right, left, x]
    stage1 = []
    for col in range(2):
        loads[col].wait()
        phased(col)
        if col == 0:
            pl.semaphore_wait(barrier, len(peers))
        stage1.append([send(y.at[col, 1 - core, xx], r1.at[col, xx], f_core) for xx in order])

    def add(dst, *others):
        total = dst[...].astype(F32)
        for other in others:
            total = total + other[...].astype(F32)
        return total

    far_sent, near_sent = [], []
    for col in range(2):
        mine = y.at[col, core]
        stage1[col][0].wait_recv()
        mine[far] = add(mine.at[far], r1.at[col, far]).astype(BF16)
        far_sent.append((
            send(mine.at[far, 0], r2a.at[col], f_right),
            send(mine.at[far, 1], r2b.at[col], f_left),
        ))
        stage1[col][1].wait_recv()
        mine[right] = add(mine.at[right], r1.at[col, right]).astype(BF16)
        stage1[col][2].wait_recv()
        to_right = send(mine.at[right, 1], rl.at[col, 1], f_right)
        mine[left] = add(mine.at[left], r1.at[col, left]).astype(BF16)
        to_left = send(mine.at[left, 0], rr.at[col, 0], f_left)
        near_sent.append([to_right, to_left])

    for col in range(2):
        mine = y.at[col, core]
        far_sent[col][0].wait_recv()
        mine[right, 0] = add(mine.at[right, 0], r2a.at[col]).astype(BF16)
        near_sent[col].append(send(mine.at[right, 0], rl.at[col, 0], f_right))
        far_sent[col][1].wait_recv()
        mine[left, 1] = add(mine.at[left, 1], r2b.at[col]).astype(BF16)
        near_sent[col].append(send(mine.at[left, 1], rr.at[col, 1], f_left))
        stage1[col][3].wait_recv()

    stage3 = []
    other = 1 - zh
    for col in range(2):
        for copy in near_sent[col]:
            copy.wait_recv()
        mine = y.at[col, core, x]
        for zz in (other, zh):
            s2[col, zz] = add(mine.at[zz], r1.at[col, x, zz], rl.at[col, zz], rr.at[col, zz]).astype(BF16)
        copies = [send(s2.at[col, other, pl.ds(0, 64)], r3.at[col], f_z)]
        for k, (zz, f_to) in enumerate(((zh, f), (other, f_z))):
            copies.append(send(s2.at[col, zz, pl.ds(64, 32)], above.at[col, k], f_to, c_prev))
            copies.append(send(s2.at[col, zz, pl.ds(96, 32)], below.at[col, k], f_to, c_next))
        stage3.append(copies)

    for load in loads[2:]:
        load.wait()

    stage5 = []
    for col in range(2):
        start = starts[col]
        side0, side1 = iota((256, 256), 0), iota((256, 256), 1)

        def matrix(source, window):
            cell = (source & 63) + jnp.where(source < 128, -HALF, SHARD) - start
            same = (lax.shift_right_logical(source, 6) & 1) == lax.shift_right_logical(window, 7)
            return jnp.where(same & (cell == (window & 127)), 1.0, 0.0).astype(BF16)

        gather_in = matrix(side0, side1)
        gather_out = matrix(side1, side0)
        for copy in stage3[col]:
            copy.wait_recv()
        main = add(s2.at[col, zh, pl.ds(0, 64)], r3.at[col])
        low = add(below.at[col, 0], below.at[col, 1])
        high = add(above.at[col, 0], above.at[col, 1])
        edge = dot(jnp.concatenate([low, high], axis=1).astype(BF16), gather_in)
        edge_re = jnp.concatenate([edge[0:16, 0:128], edge[0:16, 128:256]], axis=0)
        edge_im = jnp.concatenate([edge[16:32, 0:128], edge[16:32, 128:256]], axis=0)
        window = jnp.concatenate([main[0:32] + edge_re, main[32:64] + edge_im], axis=1).astype(BF16)
        cells = dot(window, t_v[...]).astype(BF16)
        grid_v[col, 0] = cells[:, 0:XM]
        grid_v[col, 1] = cells[:, XM:2 * XM]
        weight = w_v[col].astype(F32)
        weight = jnp.concatenate([weight, weight], axis=1)
        scaled = (cells.astype(F32) * weight).astype(BF16)
        back = dot(scaled, tt_v[...]).astype(BF16)
        block = g.at[col, zh, x, core]
        block[0:32] = back[:, 0:128]
        block[32:64] = back[:, 128:256]
        packed = jnp.concatenate([
            jnp.concatenate([back[0:16, 0:128], back[16:32, 0:128]], axis=1),
            jnp.concatenate([back[0:16, 128:256], back[16:32, 128:256]], axis=1),
        ], axis=0)
        out_edge = dot(packed, gather_out).astype(BF16)
        eo[col, 0] = out_edge[:, 0:128]
        eo[col, 1] = out_edge[:, 128:256]
        home = g.at[col, zh, x, core]
        copies = [send(home.at[pl.ds(0, 64)], home.at[pl.ds(0, 64)], f_z)]
        for f_to in (f, f_z):
            copies.append(send(eo.at[col, 0], home.at[pl.ds(96, 32)], f_to, c_prev))
            copies.append(send(eo.at[col, 1], home.at[pl.ds(64, 32)], f_to, c_next))
        stage5.append(copies)

    grid_copy = pltpu.make_async_copy(grid_v, grid_out, local_sem.at[5])
    grid_copy.start()

    stage6 = []
    for col in range(2):
        for copy in stage5[col]:
            copy.wait_recv()
        block = g.at[col, :, x, core]
        stage6.append([send(block, block, f_right), send(block, block, f_left), send(block, block, f_core)])

    stage7, to_core = [], []
    for col in range(2):
        stage6[col][0].wait_recv()
        block = g.at[col, 0, left, core]
        onward = [send(block, block, f_right)]
        block = g.at[col, :, left, core]
        to_core.append([stage6[col][2], send(block, block, f_core)])
        stage6[col][1].wait_recv()
        block = g.at[col, 1, right, core]
        onward.append(send(block, block, f_left))
        block = g.at[col, :, right, core]
        to_core[col].append(send(block, block, f_core))
        stage7.append(onward)

    outs = []
    for col in range(2):
        for copy in stage7[col]:
            copy.wait_recv()
        block = g.at[col, :, far, core]
        to_core[col].append(send(block, block, f_core))
        for copy in to_core[col]:
            copy.wait_recv()
        out = pltpu.make_async_copy(g.at[col], u_out.at[col], local_sem.at[6 + col])
        out.start()
        outs.append(out)

    for copy in sends:
        copy.wait_send()
    grid_copy.wait()
    for out in outs:
        out.wait()


N_SENDS = 8 + 4 + 4 + 4 + 10 + 10 + 6 + 8 + 2


def exchange(offsets, column_index, subgrid_offsets, spectra, weights):
    table, table_t = tables()
    any_space = pl.BlockSpec(memory_space=pl.ANY)
    hbm = pl.BlockSpec(memory_space=pltpu.HBM)
    smem = pl.BlockSpec(memory_space=pltpu.SMEM)
    return pl.pallas_call(
        exchange_kernel,
        out_shape=(
            jax.ShapeDtypeStruct((2, 2, 32, XM), BF16),
            jax.ShapeDtypeStruct((2, 2, 4, 2, 128, 128), BF16),
        ),
        in_specs=[smem, smem, smem, hbm, hbm, hbm, hbm],
        out_specs=(any_space, any_space),
        scratch_shapes=[
            pltpu.VMEM((2, 2, XM, SHARD), BF16),
            pltpu.VMEM((2, 32, XM), BF16),
            pltpu.VMEM((256, 1024), BF16),
            pltpu.VMEM((1024, 256), BF16),
            pltpu.VMEM((2, 2, 4, 2, 128, 128), BF16),
            pltpu.VMEM((2, 4, 2, 128, 128), BF16),
            pltpu.VMEM((2, 128, 128), BF16),
            pltpu.VMEM((2, 128, 128), BF16),
            pltpu.VMEM((2, 2, 128, 128), BF16),
            pltpu.VMEM((2, 2, 128, 128), BF16),
            pltpu.VMEM((2, 2, 128, 128), BF16),
            pltpu.VMEM((2, 64, 128), BF16),
            pltpu.VMEM((2, 2, 32, 128), BF16),
            pltpu.VMEM((2, 2, 32, 128), BF16),
            pltpu.VMEM((2, 2, 32, 128), BF16),
            pltpu.VMEM((2, 2, 4, 2, 128, 128), BF16),
            pltpu.VMEM((2, 2, 32, XM), BF16),
            pltpu.SemaphoreType.DMA((8,)),
            pltpu.SemaphoreType.DMA((N_SENDS,)),
            pltpu.SemaphoreType.DMA((N_SENDS,)),
        ],
        compiler_params=pltpu.CompilerParams(
            collective_id=0, has_side_effects=True
        ),
        name="exchange",
    )(offsets, column_index, subgrid_offsets, spectra, weights, jnp.asarray(table), jnp.asarray(table_t))


def place_kernel(offs_ref, colidx_ref, sub_ref, here_ref, u_ref, grid_ref, out_ref, grid_out):
    col = pl.program_id(0)
    c = here_ref[0]
    grid_out[...] = grid_ref[...]
    out_ref[...] = jnp.zeros_like(out_ref)
    position = lax.shift_right_arithmetic(sub_ref[col], 2)
    start = position - c * SHARD - HALF
    base = jnp.clip(lax.shift_right_arithmetic(start, 7), 0, SHARD // 128 - 2) * 128
    column_pos = colidx_ref[col] * XA
    first, second = offs_ref[0, 0], offs_ref[0, 1]
    cosine, sine = phase(turns(column_pos, first, second, c * SHARD + base + iota((8, 256), 1)))
    cosine, sine = cosine[0:1], sine[0:1]
    spot = iota((8, 128), 1)
    spot = c * SHARD + jnp.where(spot < HALF, spot, SHARD - 128 + spot)
    cosine_e, sine_e = phase(turns(column_pos, first, second, spot))
    cosine_e, sine_e = cosine_e[0:1], sine_e[0:1]
    put = (iota((128, 256), 1) + base == iota((128, 256), 0) + start).astype(F32).astype(BF16)
    lane = iota((16, 128), 1)
    wide = iota((32, 128), 1) < HALF
    blocks = u_ref.shape[2]
    tiles = pl.ds(pl.multiple_of(base, 128), 256)
    for xx in range(blocks):
        for cc in range(2):
            block = u_ref.at[0, 0, xx, cc]
            rows = pl.ds((xx * 2 + cc) * 32, 32)
            low_re, low_im = block[64:80].astype(F32), block[80:96].astype(F32)
            top_re, top_im = block[96:112].astype(F32), block[112:128].astype(F32)
            edges = []
            for low, top in ((low_re, top_re), (low_im, top_im)):
                edges.append(jnp.concatenate([
                    jnp.where(lane < HALF, low, pltpu.roll(top, 64, 1)),
                    jnp.where(lane < HALF, pltpu.roll(low, 64, 1), top),
                ], axis=0))
            edge_re = edges[0] * cosine_e - edges[1] * sine_e
            edge_im = edges[1] * cosine_e + edges[0] * sine_e
            zero = jnp.zeros_like(edge_re)
            for part, edge in ((0, edge_re), (1, edge_im)):
                out_ref[0, part, rows, 0:128] = jnp.where(wide, edge, zero).astype(BF16)
                out_ref[0, part, rows, SHARD - 128:SHARD] = jnp.where(wide, zero, edge).astype(BF16)
            moved = dot(block[0:64], put)
            main_re, main_im = moved[0:32], moved[32:64]
            out_re = main_re * cosine - main_im * sine
            out_im = main_im * cosine + main_re * sine
            for part, value in ((0, out_re), (1, out_im)):
                out_ref[0, part, rows, tiles] = (out_ref[0, part, rows, tiles].astype(F32) + value).astype(BF16)


def place(offsets, column_index, subgrid_offsets, here, gathered, grids):
    smem = pl.BlockSpec(memory_space=pltpu.SMEM)
    return pl.pallas_call(
        place_kernel,
        grid=(2, 2),
        out_shape=(
            jax.ShapeDtypeStruct((2, 2, XM, SHARD), BF16),
            jax.ShapeDtypeStruct((2, 2, 32, XM), BF16),
        ),
        in_specs=[
            smem, smem, smem, smem,
            pl.BlockSpec((1, 1, 4, 2, 128, 128), lambda i, j: (i, j, 0, 0, 0, 0)),
            pl.BlockSpec((1, 2, 32, XM), lambda i, j: (i, 0, 0, 0)),
        ],
        out_specs=(
            pl.BlockSpec((1, 2, XM // 2, SHARD), lambda i, j: (i, 0, j, 0)),
            pl.BlockSpec((1, 2, 32, XM), lambda i, j: (i, 0, 0, 0)),
        ),
        compiler_params=pltpu.CompilerParams(dimension_semantics=("arbitrary", "arbitrary")),
        name="place",
    )(offsets, column_index, subgrid_offsets, here, gathered, grids)


def per_device(facet_spectra, facet_offsets, column_index, subgrid_offsets, weights):
    spectra = facet_spectra.reshape(2, 2, XM, SHARD)
    subgrid_offsets = subgrid_offsets.reshape(2)
    grids, gathered = exchange(
        facet_offsets, column_index, subgrid_offsets, spectra, weights.reshape(2, 32, XM)
    )
    here = lax.axis_index("col").astype(I32).reshape(1)
    updates, grids = place(facet_offsets, column_index, subgrid_offsets, here, gathered, grids)
    return grids.reshape(2, 1, 2, 32, XM), updates.reshape(2, 1, 2, XM, SHARD)


def solution(mesh):
    in_specs = (
        P(None, "facet", None, None, "col"),
        P("facet", None),
        P(),
        P(None, "col"),
        P(None, "col", "facet", None),
    )
    out_specs = (P(None, "col", None, "facet", None), P(None, "facet", None, None, "col"))
    return jax.shard_map(
        per_device, mesh=mesh, in_specs=in_specs, out_specs=out_specs, check_vma=False
    )
```

```python
import math

import jax
import jax.numpy as jnp
import numpy as np
from jax import lax
from jax.experimental import pallas as pl
from jax.experimental.pallas import tpu as pltpu
from jax.sharding import PartitionSpec as P

XM = 512
WM = 128
XA = 448
SHARD = 1024
HALF = WM // 2
FACETS = 16
F32 = jnp.float32
BF16 = jnp.bfloat16
I32 = jnp.int32
MESH = pl.DeviceIdType.MESH


def tables():
    place = np.arange(WM)
    cell = np.arange(XM)
    turns = (place[:, None] - WM // 2) * (cell[None, :] - XM // 2) % XM
    angle = 2.0 * math.pi * turns / XM
    relative = (place + 0.5 - WM / 2.0) / (WM / 2.0)
    taper = (0.3 + 0.7 * (1.0 - relative * relative)) / math.sqrt(WM * FACETS)
    real = (taper[:, None] * np.cos(angle)).astype(np.float32)
    imag = (taper[:, None] * np.sin(angle)).astype(np.float32)
    wide = np.concatenate([real, imag], axis=1)
    tall = np.concatenate([real.T, imag.T], axis=1)
    return wide.astype(BF16), np.ascontiguousarray(tall).astype(BF16)


def phase(turn):
    quarter = lax.shift_right_logical(turn + 8192, 14)
    angle = (turn - quarter * 16384).astype(F32) * (2.0 * math.pi / 65536.0)
    square = angle * angle
    sine = angle * (
        1.0 + square * (-1.0 / 6.0 + square * (1.0 / 120.0 + square * (-1.0 / 5040.0 + square * (1.0 / 362880.0))))
    )
    cosine = 1.0 + square * (-0.5 + square * (1.0 / 24.0 + square * (-1.0 / 720.0 + square * (1.0 / 40320.0))))
    odd = (quarter & 1) == 1
    first = jnp.where(odd, sine, cosine)
    second = jnp.where(odd, cosine, sine)
    cosine = jnp.where(((quarter + 1) & 2) == 2, -first, first)
    sine = jnp.where((quarter & 2) == 2, -second, second)
    return cosine, sine


def turns(column_pos, first, second, k):
    return (column_pos * first + 4 * (k * second)) & 65535


def iota(shape, dim):
    return lax.broadcasted_iota(I32, shape, dim)


def dot(a, b):
    return jnp.dot(a, b, preferred_element_type=F32)


def exchange_kernel(
    offs_hbm, colidx_hbm, sub_hbm, x_hbm, w_hbm, t_hbm, tt_hbm,
    grid_out, g,
    offs_ref, colidx_ref, sub_ref, x_v, w_v, t_v, tt_v, y, r1, rx, s2, r3, above, below, eo,
    grid_v, local_sem, ss, rs,
):
    f = lax.axis_index("facet")
    c = lax.axis_index("col")
    core = f % 2
    x = (f // 2) % 4
    zh = f // 8
    z_lo = c % 4
    c_prev = (c + 15) % 16
    c_next = (c + 1) % 16
    zh_prev = jnp.where(z_lo == 0, 1 - zh, zh)
    zh_next = jnp.where(z_lo == 3, 1 - zh, zh)

    def facet(half, place_x, which):
        return half * 8 + place_x * 2 + which

    def x_of(d):
        return (x + d) % 4

    f_core = facet(zh, x, 1 - core)
    f_z = facet(1 - zh, x, core)
    f_x = [f] + [facet(zh, x_of(d), core) for d in (1, 2, 3)]

    barrier = pltpu.get_barrier_semaphore()
    peers = [(f_core, c), (f_z, c), (f_x[1], c), (f_x[2], c), (f_x[3], c)]
    peers += [(f, c_prev), (f_z, c_prev), (f, c_next), (f_z, c_next)]
    peers += [(facet(zh_prev, x_of(d), core), c_prev) for d in (1, 2, 3)]
    peers += [(facet(zh_next, x_of(d), core), c_next) for d in (1, 2, 3)]
    for peer in peers:
        pl.semaphore_signal(barrier, inc=1, device_id=peer, device_id_type=MESH)

    loads = [
        pltpu.make_async_copy(x_hbm.at[0], x_v.at[0], local_sem.at[0]),
        pltpu.make_async_copy(x_hbm.at[1], x_v.at[1], local_sem.at[1]),
        pltpu.make_async_copy(t_hbm, t_v, local_sem.at[2]),
        pltpu.make_async_copy(tt_hbm, tt_v, local_sem.at[3]),
        pltpu.make_async_copy(w_hbm, w_v.at[zh], local_sem.at[4]),
    ]
    scalars = [
        pltpu.make_async_copy(source, target, local_sem.at[6 + index])
        for index, (source, target) in enumerate(
            ((offs_hbm, offs_ref), (colidx_hbm, colidx_ref), (sub_hbm, sub_ref))
        )
    ]
    for load in scalars:
        load.start()
    loads[0].start()

    sends = []

    def send(src, dst, f_to, c_to=None):
        index = len(sends)
        copy = pltpu.make_async_remote_copy(
            src_ref=src, dst_ref=dst, send_sem=ss.at[index], recv_sem=rs.at[index],
            device_id=(f_to, c if c_to is None else c_to), device_id_type=MESH,
        )
        copy.start()
        sends.append(copy)
        return copy

    for load in scalars:
        load.wait()
    lane = iota((16, 128), 1)
    first, second = offs_ref[0, 0], offs_ref[0, 1]
    starts = []
    for col in range(2):
        starts.append(lax.shift_right_arithmetic(sub_ref[col], 2) - c * SHARD - HALF)

    def phased(col):
        start = starts[col]
        column_pos = colidx_ref[col] * XA
        cosine, sine = phase(turns(column_pos, first, second, c * SHARD + start + iota((8, 128), 1)))
        cosine, sine = cosine[0:1], sine[0:1]
        spot = iota((8, 128), 1)
        spot = c * SHARD + jnp.where(spot < HALF, spot, SHARD - 128 + spot)
        cosine_e, sine_e = phase(turns(column_pos, first, second, spot))
        cosine_e, sine_e = cosine_e[0:1], sine_e[0:1]
        tile = jnp.clip(lax.shift_right_arithmetic(start, 7), 0, SHARD // 128 - 2)
        pick = (iota((256, 128), 0) + tile * 128 == iota((256, 128), 1) + start).astype(F32).astype(BF16)
        bits = [(jnp.full((128, 128), 0, I32) + tile) & (1 << bit) != 0 for bit in range(3)]
        wide = iota((128, 128), 1) < HALF

        def rows(q, carry):
            span = pl.ds(pl.multiple_of(q * 128, 128), 128)
            pairs = []
            for part in range(2):
                tiles = [x_v[col, part, span, 128 * i:128 * i + 128] for i in range(8)]
                for bit, width in ((2, 5), (1, 3), (0, 2)):
                    far = 1 << bit
                    tiles = [
                        jnp.where(bits[bit], tiles[i + far], tiles[i]) if i + far < len(tiles) else tiles[i]
                        for i in range(width)
                    ]
                pairs.append(jnp.concatenate(tiles, axis=1))
            main_re = dot(pairs[0], pick)
            main_im = dot(pairs[1], pick)
            out_re = (main_re * cosine + main_im * sine).astype(BF16)
            out_im = (main_im * cosine - main_re * sine).astype(BF16)
            edge_re = jnp.where(wide, x_v[col, 0, span, 0:128].astype(F32), x_v[col, 0, span, SHARD - 128:SHARD].astype(F32))
            edge_im = jnp.where(wide, x_v[col, 1, span, 0:128].astype(F32), x_v[col, 1, span, SHARD - 128:SHARD].astype(F32))
            e_re = edge_re * cosine_e + edge_im * sine_e
            e_im = edge_im * cosine_e - edge_re * sine_e
            swap_re = pltpu.roll(e_re, 64, 1)
            swap_im = pltpu.roll(e_im, 64, 1)
            for j in range(4):
                xx, cc = (q % 2) * 2 + j // 2, j % 2
                block = y.at[col, cc, xx, q // 2]
                a, b, d = 32 * j, 32 * j + 16, 32 * j + 32
                block[0:32] = out_re[a:d]
                block[32:64] = out_im[a:d]
                block[64:80] = jnp.where(lane < HALF, e_re[a:b], swap_re[b:d]).astype(BF16)
                block[80:96] = jnp.where(lane < HALF, e_im[a:b], swap_im[b:d]).astype(BF16)
                block[96:112] = jnp.where(lane < HALF, swap_re[a:b], e_re[b:d]).astype(BF16)
                block[112:128] = jnp.where(lane < HALF, swap_im[a:b], e_im[b:d]).astype(BF16)
            return carry

        lax.fori_loop(0, 4, rows, 0)

    def total(*refs):
        result = refs[0][...].astype(F32)
        for ref in refs[1:]:
            result = result + ref[...].astype(F32)
        return result

    order = (2, 1, 3, 0)
    to_core = []
    weights_there = None
    for col in range(2):
        loads[col].wait()
        for load in loads[1:2] if col == 0 else loads[2:]:
            load.start()
        phased(col)
        if col == 0:
            pl.semaphore_wait(barrier, len(peers))
        to_core.append([send(y.at[col, 1 - core, x_of(d)], r1.at[col, x_of(d)], f_core) for d in order])
        if col == 0:
            weights_there = send(w_hbm, w_v.at[zh], f_z)

    to_x = []
    for col in range(2):
        copies = []
        for d, copy in zip(order, to_core[col]):
            copy.wait_recv()
            xx = x_of(d)
            if d:
                y[col, core, xx] = total(y.at[col, core, xx], r1.at[col, xx]).astype(BF16)
                copies.append(send(y.at[col, core, xx], rx.at[col, d - 1], f_x[d]))
        to_x.append(copies)

    to_z = []
    for col in range(2):
        for copy in to_x[col]:
            copy.wait_recv()
        s2[col] = total(
            y.at[col, core, x], r1.at[col, x], rx.at[col, 0], rx.at[col, 1], rx.at[col, 2]
        ).astype(BF16)
        copies = [send(s2.at[col, :, pl.ds(0, 64)], r3.at[col], f_z)]
        for k, f_to in enumerate((f, f_z)):
            copies.append(send(s2.at[col, :, pl.ds(64, 32)], above.at[col, k], f_to, c_prev))
            copies.append(send(s2.at[col, :, pl.ds(96, 32)], below.at[col, k], f_to, c_next))
        to_z.append(copies)

    for load in loads[2:]:
        load.wait()
    weights_there.wait_recv()

    to_all = []
    for col in range(2):
        start = starts[col]

        def matrix(source, window):
            cell = (source & 63) + jnp.where(source < 128, -HALF, SHARD) - start
            same = (lax.shift_right_logical(source, 6) & 1) == lax.shift_right_logical(window, 7)
            return jnp.where(same & (cell == (window & 127)), 1.0, 0.0).astype(BF16)

        side0, side1 = iota((256, 256), 0), iota((256, 256), 1)
        gather_in = matrix(side0, side1)
        gather_out = matrix(side1, side0)
        for copy in to_z[col]:
            copy.wait_recv()
        main = total(s2.at[col, :, pl.ds(0, 64)], r3.at[col])
        low = total(below.at[col, 0], below.at[col, 1]).reshape(64, 128)
        high = total(above.at[col, 0], above.at[col, 1]).reshape(64, 128)
        edge = dot(jnp.concatenate([low, high], axis=1).astype(BF16), gather_in)
        windows = []
        for part in range(2):
            for half in range(2):
                a = half * 32 + part * 16
                reach = jnp.concatenate([edge[a:a + 16, 0:128], edge[a:a + 16, 128:256]], axis=0)
                windows.append(main[half, part * 32:part * 32 + 32] + reach)
        window = jnp.concatenate(windows, axis=0).astype(BF16)
        prod = dot(window, t_v[...])
        cells_re = (prod[0:64, 0:XM] - prod[64:128, XM:2 * XM]).astype(BF16)
        cells_im = (prod[0:64, XM:2 * XM] + prod[64:128, 0:XM]).astype(BF16)
        weight = jnp.concatenate([w_v[0, col], w_v[1, col]], axis=0).astype(F32)
        scaled_re = (cells_re.astype(F32) * weight).astype(BF16)
        scaled_im = (cells_im.astype(F32) * weight).astype(BF16)
        prod = dot(jnp.concatenate([scaled_re, scaled_im], axis=0), tt_v[...])
        back_re = (prod[0:64, 0:WM] + prod[64:128, WM:2 * WM]).astype(BF16)
        back_im = (prod[64:128, 0:WM] - prod[0:64, WM:2 * WM]).astype(BF16)
        for half in range(2):
            grid_v[half, col, 0] = cells_re[half * 32:half * 32 + 32]
            grid_v[half, col, 1] = cells_im[half * 32:half * 32 + 32]
        packed = []
        for half in range(2):
            block = g.at[col, half, x, core]
            a = half * 32
            block[0:32] = back_re[a:a + 32]
            block[32:64] = back_im[a:a + 32]
            for back in (back_re, back_im):
                packed.append(jnp.concatenate([back[a:a + 16], back[a + 16:a + 32]], axis=1))
        out_edge = dot(jnp.concatenate(packed, axis=0), gather_out).astype(BF16)
        eo[col, 0] = out_edge[:, 0:128].reshape(2, 32, 128)
        eo[col, 1] = out_edge[:, 128:256].reshape(2, 32, 128)
        low, high = g.at[col, :, x, core, pl.ds(64, 32)], g.at[col, :, x, core, pl.ds(96, 32)]
        edges = []
        for d in order:
            edges.append((
                send(eo.at[col, 0], high, facet(zh_prev, x_of(d), core), c_prev),
                send(eo.at[col, 1], low, facet(zh_next, x_of(d), core), c_next),
            ))
        home = g.at[col, :, x, core, pl.ds(0, 64)]
        mains = [send(home, home, f_x[d]) for d in (2, 1, 3)]
        to_all.append((mains, edges, [send(home, home, f_core)]))

    grid_copy = pltpu.make_async_copy(grid_v.at[zh], grid_out, local_sem.at[5])
    grid_copy.start()

    for col in range(2):
        mains, edges, passed = to_all[col]
        for d, copy in ((1, mains[1]), (3, mains[2]), (2, mains[0])):
            copy.wait_recv()
            block = g.at[col, :, x_of(4 - d), core, pl.ds(0, 64)]
            passed.append(send(block, block, f_core))
        for d, pair in zip(order, edges):
            for copy in pair:
                copy.wait_recv()
            block = g.at[col, :, x_of(4 - d), core, pl.ds(64, 64)]
            passed.append(send(block, block, f_core))
    for col in range(2):
        for copy in to_all[col][2]:
            copy.wait_recv()

    for copy in sends:
        copy.wait_send()
    grid_copy.wait()


N_SENDS = 63


def exchange(offsets, column_index, subgrid_offsets, spectra, weights):
    table, table_t = tables()
    hbm = pl.BlockSpec(memory_space=pltpu.HBM)
    vmem = pl.BlockSpec(memory_space=pltpu.VMEM)
    return pl.pallas_call(
        exchange_kernel,
        out_shape=(
            pltpu.VMEM((2, 2, 32, XM), BF16),
            pltpu.VMEM((2, 2, 4, 2, 128, 128), BF16),
        ),
        in_specs=[hbm] * 7,
        out_specs=(vmem, vmem),
        scratch_shapes=[
            pltpu.SMEM((1, 2), I32),
            pltpu.SMEM((2,), I32),
            pltpu.SMEM((2,), I32),
            pltpu.VMEM((2, 2, XM, SHARD), BF16),
            pltpu.VMEM((2, 2, 32, XM), BF16),
            pltpu.VMEM((WM, 2 * XM), BF16),
            pltpu.VMEM((XM, 2 * WM), BF16),
            pltpu.VMEM((2, 2, 4, 2, 128, 128), BF16),
            pltpu.VMEM((2, 4, 2, 128, 128), BF16),
            pltpu.VMEM((2, 3, 2, 128, 128), BF16),
            pltpu.VMEM((2, 2, 128, 128), BF16),
            pltpu.VMEM((2, 2, 64, 128), BF16),
            pltpu.VMEM((2, 2, 2, 32, 128), BF16),
            pltpu.VMEM((2, 2, 2, 32, 128), BF16),
            pltpu.VMEM((2, 2, 2, 32, 128), BF16),
            pltpu.VMEM((2, 2, 2, 32, XM), BF16),
            pltpu.SemaphoreType.DMA((9,)),
            pltpu.SemaphoreType.DMA((N_SENDS,)),
            pltpu.SemaphoreType.DMA((N_SENDS,)),
        ],
        compiler_params=pltpu.CompilerParams(collective_id=0, has_side_effects=True),
        name="exchange",
    )(offsets, column_index, subgrid_offsets, spectra, weights, jnp.asarray(table), jnp.asarray(table_t))


def place_kernel(offs_ref, colidx_ref, sub_ref, here_ref, u_ref, grid_ref, out_hbm, grid_hbm, out, sem):
    grid_copy = pltpu.make_async_copy(grid_ref, grid_hbm, sem.at[0])
    grid_copy.start()
    c = here_ref[0]
    first, second = offs_ref[0, 0], offs_ref[0, 1]
    spot = iota((8, 128), 1)
    spot = c * SHARD + jnp.where(spot < HALF, spot, SHARD - 128 + spot)
    lane = iota((16, 128), 1)
    wide = iota((32, 128), 1) < HALF
    for col in range(2):
        start = lax.shift_right_arithmetic(sub_ref[col], 2) - c * SHARD - HALF
        base = jnp.clip(lax.shift_right_arithmetic(start, 7), 0, SHARD // 128 - 2) * 128
        column_pos = colidx_ref[col] * XA
        cosine, sine = phase(turns(column_pos, first, second, c * SHARD + base + iota((8, 256), 1)))
        cosine, sine = cosine[0:1], sine[0:1]
        cosine_e, sine_e = phase(turns(column_pos, first, second, spot))
        cosine_e, sine_e = cosine_e[0:1], sine_e[0:1]
        put = (iota((128, 256), 1) + base == iota((128, 256), 0) + start).astype(F32).astype(BF16)
        tiles = pl.ds(pl.multiple_of(base, 128), 256)

        def rows_of(q, carry):
            span = pl.ds(pl.multiple_of(q * 128, 128), 128)
            out[col, :, span] = jnp.zeros((2, 128, SHARD), BF16)
            for j in range(4):
                block = u_ref.at[col, q // 2, (q % 2) * 2 + j // 2, j % 2]
                rows = pl.ds(pl.multiple_of(q * 128 + 32 * j, 32), 32)
                low_re, low_im = block[64:80].astype(F32), block[80:96].astype(F32)
                top_re, top_im = block[96:112].astype(F32), block[112:128].astype(F32)
                edges = []
                for low, top in ((low_re, top_re), (low_im, top_im)):
                    edges.append(jnp.concatenate([
                        jnp.where(lane < HALF, low, pltpu.roll(top, 64, 1)),
                        jnp.where(lane < HALF, pltpu.roll(low, 64, 1), top),
                    ], axis=0))
                edge_re = edges[0] * cosine_e - edges[1] * sine_e
                edge_im = edges[1] * cosine_e + edges[0] * sine_e
                zero = jnp.zeros_like(edge_re)
                for part, edge in ((0, edge_re), (1, edge_im)):
                    out[col, part, rows, 0:128] = jnp.where(wide, edge, zero).astype(BF16)
                    out[col, part, rows, SHARD - 128:SHARD] = jnp.where(wide, zero, edge).astype(BF16)
                moved = dot(block[0:64], put)
                main_re, main_im = moved[0:32], moved[32:64]
                out_re = main_re * cosine - main_im * sine
                out_im = main_im * cosine + main_re * sine
                for part, value in ((0, out_re), (1, out_im)):
                    out[col, part, rows, tiles] = (out[col, part, rows, tiles].astype(F32) + value).astype(BF16)
            pltpu.make_async_copy(out.at[col, :, span], out_hbm.at[col, :, span], sem.at[1 + col * 4 + q]).start()
            return carry

        lax.fori_loop(0, 4, rows_of, 0)
    for col in range(2):
        for q in range(4):
            span = pl.ds(q * 128, 128)
            pltpu.make_async_copy(out.at[col, :, span], out_hbm.at[col, :, span], sem.at[1 + col * 4 + q]).wait()
    grid_copy.wait()


def place(offsets, column_index, subgrid_offsets, here, gathered, grids):
    smem = pl.BlockSpec(memory_space=pltpu.SMEM)
    hbm = pl.BlockSpec(memory_space=pltpu.HBM)
    vmem = pl.BlockSpec(memory_space=pltpu.VMEM)
    gathered = pltpu.with_memory_space_constraint(gathered, pltpu.VMEM)
    grids = pltpu.with_memory_space_constraint(grids, pltpu.VMEM)
    return pl.pallas_call(
        place_kernel,
        out_shape=(
            jax.ShapeDtypeStruct((2, 2, XM, SHARD), BF16),
            jax.ShapeDtypeStruct((2, 2, 32, XM), BF16),
        ),
        in_specs=[smem, smem, smem, smem, vmem, vmem],
        out_specs=(hbm, hbm),
        scratch_shapes=[
            pltpu.VMEM((2, 2, XM, SHARD), BF16),
            pltpu.SemaphoreType.DMA((9,)),
        ],
        compiler_params=pltpu.CompilerParams(vmem_limit_bytes=16 << 20),
        name="place",
    )(offsets, column_index, subgrid_offsets, here, gathered, grids)


def per_device(facet_spectra, facet_offsets, column_index, subgrid_offsets, weights):
    spectra = facet_spectra.reshape(2, 2, XM, SHARD)
    subgrid_offsets = subgrid_offsets.reshape(2)
    grids, gathered = exchange(
        facet_offsets, column_index, subgrid_offsets, spectra, weights.reshape(2, 32, XM)
    )
    here = lax.axis_index("col").astype(I32).reshape(1)
    updates, grids = place(facet_offsets, column_index, subgrid_offsets, here, gathered, grids)
    return grids.reshape(2, 1, 2, 32, XM), updates.reshape(2, 1, 2, XM, SHARD)


def solution(mesh):
    in_specs = (
        P(None, "facet", None, None, "col"),
        P("facet", None),
        P(),
        P(None, "col"),
        P(None, "col", "facet", None),
    )
    out_specs = (P(None, "col", None, "facet", None), P(None, "facet", None, None, "col"))
    return jax.shard_map(
        per_device, mesh=mesh, in_specs=in_specs, out_specs=out_specs, check_vma=False
    )
```

```python
import math

import jax
import jax.numpy as jnp
import numpy as np
from jax import lax
from jax.experimental import pallas as pl
from jax.experimental.pallas import tpu as pltpu
from jax.sharding import PartitionSpec as P

XM = 512
WM = 128
XA = 448
SHARD = 1024
HALF = WM // 2
FACETS = 16
F32 = jnp.float32
BF16 = jnp.bfloat16
I32 = jnp.int32
MESH = pl.DeviceIdType.MESH


def tables():
    place = np.arange(WM)
    cell = np.arange(XM)
    turns = (place[:, None] - WM // 2) * (cell[None, :] - XM // 2) % XM
    angle = 2.0 * math.pi * turns / XM
    relative = (place + 0.5 - WM / 2.0) / (WM / 2.0)
    taper = (0.3 + 0.7 * (1.0 - relative * relative)) / math.sqrt(WM * FACETS)
    real = (taper[:, None] * np.cos(angle)).astype(np.float32)
    imag = (taper[:, None] * np.sin(angle)).astype(np.float32)
    wide = np.concatenate([real, imag], axis=1)
    tall = np.concatenate([real.T, imag.T], axis=1)
    return wide.astype(BF16), np.ascontiguousarray(tall).astype(BF16)


def phase(turn):
    quarter = lax.shift_right_logical(turn + 8192, 14)
    angle = (turn - quarter * 16384).astype(F32) * (2.0 * math.pi / 65536.0)
    square = angle * angle
    sine = angle * (
        1.0 + square * (-1.0 / 6.0 + square * (1.0 / 120.0 + square * (-1.0 / 5040.0 + square * (1.0 / 362880.0))))
    )
    cosine = 1.0 + square * (-0.5 + square * (1.0 / 24.0 + square * (-1.0 / 720.0 + square * (1.0 / 40320.0))))
    odd = (quarter & 1) == 1
    first = jnp.where(odd, sine, cosine)
    second = jnp.where(odd, cosine, sine)
    cosine = jnp.where(((quarter + 1) & 2) == 2, -first, first)
    sine = jnp.where((quarter & 2) == 2, -second, second)
    return cosine, sine


def turns(column_pos, first, second, k):
    return (column_pos * first + 4 * (k * second)) & 65535


def iota(shape, dim):
    return lax.broadcasted_iota(I32, shape, dim)


def dot(a, b):
    return jnp.dot(a, b, preferred_element_type=F32)


def exchange_kernel(
    offs_hbm, colidx_hbm, sub_hbm, x_hbm, w_hbm, t_hbm, tt_hbm,
    grid_out, g,
    offs_ref, colidx_ref, sub_ref, x_v, w_v, t_v, tt_v, y, r1, rx, s2, rz, eo,
    grid_v, local_sem, ss, rs,
):
    f = lax.axis_index("facet")
    c = lax.axis_index("col")
    core = f % 2
    x = (f // 2) % 4
    zh = f // 8
    z_lo = c % 4
    c_prev = (c + 15) % 16
    c_next = (c + 1) % 16
    zh_prev = jnp.where(z_lo == 0, 1 - zh, zh)
    zh_next = jnp.where(z_lo == 3, 1 - zh, zh)

    def facet(half, place_x, which):
        return half * 8 + place_x * 2 + which

    def x_of(d):
        return (x + d) % 4

    f_core = facet(zh, x, 1 - core)
    f_z = facet(1 - zh, x, core)
    f_x = [f] + [facet(zh, x_of(d), core) for d in (1, 2, 3)]

    barrier = pltpu.get_barrier_semaphore()
    peers = [(f_core, c), (f_z, c), (f_x[1], c), (f_x[2], c), (f_x[3], c)]
    peers += [(f, c_prev), (f_z, c_prev), (f, c_next), (f_z, c_next)]
    peers += [(facet(zh_prev, x_of(d), core), c_prev) for d in (1, 2, 3)]
    peers += [(facet(zh_next, x_of(d), core), c_next) for d in (1, 2, 3)]
    for peer in peers:
        pl.semaphore_signal(barrier, inc=1, device_id=peer, device_id_type=MESH)

    loads = [
        pltpu.make_async_copy(t_hbm, t_v, local_sem.at[2]),
        pltpu.make_async_copy(tt_hbm, tt_v, local_sem.at[3]),
        pltpu.make_async_copy(w_hbm, w_v.at[zh], local_sem.at[4]),
    ]
    spectra = [
        [
            pltpu.make_async_copy(
                x_hbm.at[col, part, pl.ds(256 * half, 256)],
                x_v.at[col, part, pl.ds(256 * half, 256)],
                local_sem.at[col],
            )
            for half in range(2) for part in range(2)
        ]
        for col in range(2)
    ]
    scalars = [
        pltpu.make_async_copy(source, target, local_sem.at[6 + index])
        for index, (source, target) in enumerate(
            ((offs_hbm, offs_ref), (colidx_hbm, colidx_ref), (sub_hbm, sub_ref))
        )
    ]
    for load in scalars:
        load.start()
    for load in spectra[0]:
        load.start()

    used = []

    def group():
        used.append(None)
        return rs.at[len(used) - 1]

    sent = []

    def send(src, dst, arrived, f_to, c_to=None):
        sent.append(math.prod(src.shape))
        pltpu.make_async_remote_copy(
            src_ref=src, dst_ref=dst, send_sem=ss.at[0], recv_sem=arrived,
            device_id=(f_to, c if c_to is None else c_to), device_id_type=MESH,
        ).start()

    def arrive(whole, arrived):
        pltpu.make_async_copy(whole, whole, arrived).wait()

    for load in scalars:
        load.wait()
    lane = iota((16, 128), 1)
    first, second = offs_ref[0, 0], offs_ref[0, 1]
    starts = []
    for col in range(2):
        starts.append(lax.shift_right_arithmetic(sub_ref[col], 2) - c * SHARD - HALF)

    def phased(col):
        start = starts[col]
        column_pos = colidx_ref[col] * XA
        cosine, sine = phase(turns(column_pos, first, second, c * SHARD + start + iota((8, 128), 1)))
        cosine, sine = cosine[0:1], sine[0:1]
        spot = iota((8, 128), 1)
        spot = c * SHARD + jnp.where(spot < HALF, spot, SHARD - 128 + spot)
        cosine_e, sine_e = phase(turns(column_pos, first, second, spot))
        cosine_e, sine_e = cosine_e[0:1], sine_e[0:1]
        tile = jnp.clip(lax.shift_right_arithmetic(start, 7), 0, SHARD // 128 - 2)
        pick = (iota((256, 128), 0) + tile * 128 == iota((256, 128), 1) + start).astype(F32).astype(BF16)
        bits = [(jnp.full((128, 128), 0, I32) + tile) & (1 << bit) != 0 for bit in range(3)]
        wide = iota((128, 128), 1) < HALF

        for q in range(4):
            span = pl.ds(q * 128, 128)
            pairs = []
            for part in range(2):
                tiles = [x_v[col, part, span, 128 * i:128 * i + 128] for i in range(8)]
                for bit, width in ((2, 5), (1, 3), (0, 2)):
                    far = 1 << bit
                    tiles = [
                        jnp.where(bits[bit], tiles[i + far], tiles[i]) if i + far < len(tiles) else tiles[i]
                        for i in range(width)
                    ]
                pairs.append(jnp.concatenate(tiles, axis=1))
            main_re = dot(pairs[0], pick)
            main_im = dot(pairs[1], pick)
            out_re = (main_re * cosine + main_im * sine).astype(BF16)
            out_im = (main_im * cosine - main_re * sine).astype(BF16)
            edge_re = jnp.where(wide, x_v[col, 0, span, 0:128].astype(F32), x_v[col, 0, span, SHARD - 128:SHARD].astype(F32))
            edge_im = jnp.where(wide, x_v[col, 1, span, 0:128].astype(F32), x_v[col, 1, span, SHARD - 128:SHARD].astype(F32))
            e_re = edge_re * cosine_e + edge_im * sine_e
            e_im = edge_im * cosine_e - edge_re * sine_e
            swap_re = pltpu.roll(e_re, 64, 1)
            swap_im = pltpu.roll(e_im, 64, 1)
            for j in range(4):
                xx, cc = (q % 2) * 2 + j // 2, j % 2
                block = y.at[col, cc, xx, q // 2]
                a, b, d = 32 * j, 32 * j + 16, 32 * j + 32
                block[0:32] = out_re[a:d]
                block[32:64] = out_im[a:d]
                block[64:80] = jnp.where(lane < HALF, e_re[a:b], swap_re[b:d]).astype(BF16)
                block[80:96] = jnp.where(lane < HALF, e_im[a:b], swap_im[b:d]).astype(BF16)
                block[96:112] = jnp.where(lane < HALF, swap_re[a:b], e_re[b:d]).astype(BF16)
                block[112:128] = jnp.where(lane < HALF, swap_im[a:b], e_im[b:d]).astype(BF16)

    def total(*refs):
        result = refs[0][...].astype(F32)
        for ref in refs[1:]:
            result = result + ref[...].astype(F32)
        return result

    order = (2, 1, 3, 0)
    from_core = [group() for _ in range(2)]
    from_z_weights = group()
    for col in range(2):
        arrive(x_v.at[col], local_sem.at[col])
        for load in spectra[1] if col == 0 else loads:
            load.start()
        phased(col)
        if col == 0:
            pl.semaphore_wait(barrier, len(peers))
        send(y.at[col, 1 - core], r1.at[col], from_core[col], f_core)
    send(w_hbm, w_v.at[zh], from_z_weights, f_z)

    from_x = [group() for _ in range(2)]
    for col in range(2):
        arrive(r1.at[col], from_core[col])
        for d in order[:3]:
            xx = x_of(d)
            y[col, core, xx] = total(y.at[col, core, xx], r1.at[col, xx]).astype(BF16)
            send(y.at[col, core, xx], rx.at[col, d - 1], from_x[col], f_x[d])

    from_z = [group() for _ in range(2)]
    for col in range(2):
        arrive(rx.at[col], from_x[col])
        s2[col] = total(
            y.at[col, core, x], r1.at[col, x], rx.at[col, 0], rx.at[col, 1], rx.at[col, 2]
        ).astype(BF16)
        send(s2.at[col, :, pl.ds(0, 64)], rz.at[col, pl.ds(4, 2)], from_z[col], f_z)
        for k, f_to in enumerate((f_z, f)):
            for side, c_to in enumerate((c_next, c_prev)):
                send(
                    s2.at[col, :, pl.ds(96 - 32 * side, 32)],
                    rz.at[col, pl.ds(2 * side, 2), pl.ds(32 * k, 32)],
                    from_z[col], f_to, c_to,
                )

    for load in loads:
        load.wait()
    arrive(w_v.at[1 - zh], from_z_weights)

    from_mains = [[group() for _ in range(3)] for _ in range(2)]
    from_edges = [[group() for _ in range(4)] for _ in range(2)]
    passed = [[group() for _ in range(2)] for _ in range(2)]
    for col in range(2):
        start = starts[col]

        def matrix(source, window):
            cell = (source & 63) + jnp.where(source < 128, -HALF, SHARD) - start
            same = (lax.shift_right_logical(source, 6) & 1) == lax.shift_right_logical(window, 7)
            return jnp.where(same & (cell == (window & 127)), 1.0, 0.0).astype(BF16)

        side0, side1 = iota((256, 256), 0), iota((256, 256), 1)
        gather_in = matrix(side0, side1)
        gather_out = matrix(side1, side0)
        arrive(rz.at[col], from_z[col])
        main = total(s2.at[col, :, pl.ds(0, 64)], rz.at[col, pl.ds(4, 2)])
        low, high = (
            total(
                rz.at[col, pl.ds(2 * side, 2), pl.ds(0, 32)], rz.at[col, pl.ds(2 * side, 2), pl.ds(32, 32)]
            ).reshape(64, 128)
            for side in range(2)
        )
        edge = dot(jnp.concatenate([low, high], axis=1).astype(BF16), gather_in)
        windows = []
        for part in range(2):
            for half in range(2):
                a = half * 32 + part * 16
                reach = jnp.concatenate([edge[a:a + 16, 0:128], edge[a:a + 16, 128:256]], axis=0)
                windows.append(main[half, part * 32:part * 32 + 32] + reach)
        window = jnp.concatenate(windows, axis=0).astype(BF16)
        prod = dot(window, t_v[...])
        cells_re = (prod[0:64, 0:XM] - prod[64:128, XM:2 * XM]).astype(BF16)
        cells_im = (prod[0:64, XM:2 * XM] + prod[64:128, 0:XM]).astype(BF16)
        weight = jnp.concatenate([w_v[0, col], w_v[1, col]], axis=0).astype(F32)
        scaled_re = (cells_re.astype(F32) * weight).astype(BF16)
        scaled_im = (cells_im.astype(F32) * weight).astype(BF16)
        prod = dot(jnp.concatenate([scaled_re, scaled_im], axis=0), tt_v[...])
        back_re = (prod[0:64, 0:WM] + prod[64:128, WM:2 * WM]).astype(BF16)
        back_im = (prod[64:128, 0:WM] - prod[0:64, WM:2 * WM]).astype(BF16)
        for half in range(2):
            grid_v[half, col, 0] = cells_re[half * 32:half * 32 + 32]
            grid_v[half, col, 1] = cells_im[half * 32:half * 32 + 32]
        packed = []
        for half in range(2):
            block = g.at[col, half, x, core]
            a = half * 32
            block[0:32] = back_re[a:a + 32]
            block[32:64] = back_im[a:a + 32]
            for back in (back_re, back_im):
                packed.append(jnp.concatenate([back[a:a + 16], back[a + 16:a + 32]], axis=1))
        out_edge = dot(jnp.concatenate(packed, axis=0), gather_out).astype(BF16)
        eo[col, 0] = out_edge[:, 0:128].reshape(2, 32, 128)
        eo[col, 1] = out_edge[:, 128:256].reshape(2, 32, 128)
        low, high = g.at[col, :, x, core, pl.ds(64, 32)], g.at[col, :, x, core, pl.ds(96, 32)]
        for d in order:
            send(eo.at[col, 0], high, from_edges[col][d], facet(zh_prev, x_of(d), core), c_prev)
            send(eo.at[col, 1], low, from_edges[col][d], facet(zh_next, x_of(d), core), c_next)
        home = g.at[col, :, x, core, pl.ds(0, 64)]
        for d in (2, 1, 3):
            send(home, home, from_mains[col][d - 1], f_x[d])
        send(home, home, passed[col][0], f_core)

    grid_copy = pltpu.make_async_copy(grid_v.at[zh], grid_out, local_sem.at[5])
    grid_copy.start()

    for col in range(2):
        for d in (1, 3, 2):
            block = g.at[col, :, x_of(4 - d), core, pl.ds(0, 64)]
            arrive(block, from_mains[col][d - 1])
            send(block, block, passed[col][0], f_core)
        for d in order:
            block = g.at[col, :, x_of(4 - d), core, pl.ds(64, 64)]
            arrive(block, from_edges[col][d])
            send(block, block, passed[col][1], f_core)
    for col in range(2):
        for half in range(2):
            arrive(g.at[col, :, :, 1 - core, pl.ds(64 * half, 64)], passed[col][half])

    assert len(used) == N_GROUPS
    every = sum(sent) // SHARD
    arrive(x_v.reshape(2 * 2 * XM, SHARD).at[pl.ds(0, every)], ss.at[0])
    grid_copy.wait()


N_GROUPS = 25


def exchange(offsets, column_index, subgrid_offsets, spectra, weights):
    table, table_t = tables()
    hbm = pl.BlockSpec(memory_space=pltpu.HBM)
    vmem = pl.BlockSpec(memory_space=pltpu.VMEM)
    return pl.pallas_call(
        exchange_kernel,
        out_shape=(
            pltpu.VMEM((2, 2, 32, XM), BF16),
            pltpu.VMEM((2, 2, 4, 2, 128, 128), BF16),
        ),
        in_specs=[hbm] * 7,
        out_specs=(vmem, vmem),
        scratch_shapes=[
            pltpu.SMEM((1, 2), I32),
            pltpu.SMEM((2,), I32),
            pltpu.SMEM((2,), I32),
            pltpu.VMEM((2, 2, XM, SHARD), BF16),
            pltpu.VMEM((2, 2, 32, XM), BF16),
            pltpu.VMEM((WM, 2 * XM), BF16),
            pltpu.VMEM((XM, 2 * WM), BF16),
            pltpu.VMEM((2, 2, 4, 2, 128, 128), BF16),
            pltpu.VMEM((2, 4, 2, 128, 128), BF16),
            pltpu.VMEM((2, 3, 2, 128, 128), BF16),
            pltpu.VMEM((2, 2, 128, 128), BF16),
            pltpu.VMEM((2, 6, 64, 128), BF16),
            pltpu.VMEM((2, 2, 2, 32, 128), BF16),
            pltpu.VMEM((2, 2, 2, 32, XM), BF16),
            pltpu.SemaphoreType.DMA((9,)),
            pltpu.SemaphoreType.DMA((1,)),
            pltpu.SemaphoreType.DMA((N_GROUPS,)),
        ],
        compiler_params=pltpu.CompilerParams(collective_id=0, has_side_effects=True),
        name="exchange",
    )(offsets, column_index, subgrid_offsets, spectra, weights, jnp.asarray(table), jnp.asarray(table_t))


def place_kernel(offs_hbm, colidx_hbm, sub_hbm, u_ref, grid_ref, out_hbm, grid_hbm, offs_ref, colidx_ref, sub_ref, out, sem):
    grid_copy = pltpu.make_async_copy(grid_ref, grid_hbm, sem.at[0])
    grid_copy.start()
    scalars = [
        pltpu.make_async_copy(source, target, sem.at[9 + index])
        for index, (source, target) in enumerate(
            ((offs_hbm, offs_ref), (colidx_hbm, colidx_ref), (sub_hbm, sub_ref))
        )
    ]
    for load in scalars:
        load.start()
    for col in range(2):
        out[col] = jnp.zeros((2, XM, SHARD), BF16)
    for load in scalars:
        load.wait()
    c = lax.axis_index("col")
    first, second = offs_ref[0, 0], offs_ref[0, 1]
    spot = iota((8, 128), 1)
    spot = c * SHARD + jnp.where(spot < HALF, spot, SHARD - 128 + spot)
    lane = iota((16, 128), 1)
    wide = iota((32, 128), 1) < HALF
    for col in range(2):
        start = lax.shift_right_arithmetic(sub_ref[col], 2) - c * SHARD - HALF
        base = jnp.clip(lax.shift_right_arithmetic(start, 7), 0, SHARD // 128 - 2) * 128
        column_pos = colidx_ref[col] * XA
        cosine, sine = phase(turns(column_pos, first, second, c * SHARD + base + iota((8, 256), 1)))
        cosine, sine = cosine[0:1], sine[0:1]
        cosine_e, sine_e = phase(turns(column_pos, first, second, spot))
        cosine_e, sine_e = cosine_e[0:1], sine_e[0:1]
        put = (iota((128, 256), 1) + base == iota((128, 256), 0) + start).astype(F32).astype(BF16)
        tiles = pl.ds(pl.multiple_of(base, 128), 256)

        for q in range(4):
            span = pl.ds(q * 128, 128)
            some = u_ref.at[col, q // 2, pl.ds((q % 2) * 2, 2)]
            moved = dot(some[:, :, 0:64].reshape(256, 128), put)
            for j in range(4):
                block = some.at[j // 2, j % 2]
                rows = pl.ds(q * 128 + 32 * j, 32)
                low_re, low_im = block[64:80].astype(F32), block[80:96].astype(F32)
                top_re, top_im = block[96:112].astype(F32), block[112:128].astype(F32)
                edges = []
                for low, top in ((low_re, top_re), (low_im, top_im)):
                    edges.append(jnp.concatenate([
                        jnp.where(lane < HALF, low, pltpu.roll(top, 64, 1)),
                        jnp.where(lane < HALF, pltpu.roll(low, 64, 1), top),
                    ], axis=0))
                edge_re = edges[0] * cosine_e - edges[1] * sine_e
                edge_im = edges[1] * cosine_e + edges[0] * sine_e
                zero = jnp.zeros_like(edge_re)
                for part, edge in ((0, edge_re), (1, edge_im)):
                    out[col, part, rows, 0:128] = jnp.where(wide, edge, zero).astype(BF16)
                    out[col, part, rows, SHARD - 128:SHARD] = jnp.where(wide, zero, edge).astype(BF16)
                main_re, main_im = moved[64 * j:64 * j + 32], moved[64 * j + 32:64 * j + 64]
                out_re = main_re * cosine - main_im * sine
                out_im = main_im * cosine + main_re * sine
                for part, value in ((0, out_re), (1, out_im)):
                    out[col, part, rows, tiles] = (out[col, part, rows, tiles].astype(F32) + value).astype(BF16)
            pltpu.make_async_copy(out.at[col, :, span], out_hbm.at[col, :, span], sem.at[1 + col * 4 + q]).start()

    for col in range(2):
        for q in range(4):
            span = pl.ds(q * 128, 128)
            pltpu.make_async_copy(out.at[col, :, span], out_hbm.at[col, :, span], sem.at[1 + col * 4 + q]).wait()
    grid_copy.wait()


def place(offsets, column_index, subgrid_offsets, gathered, grids):
    hbm = pl.BlockSpec(memory_space=pltpu.HBM)
    vmem = pl.BlockSpec(memory_space=pltpu.VMEM)
    gathered = pltpu.with_memory_space_constraint(gathered, pltpu.VMEM)
    grids = pltpu.with_memory_space_constraint(grids, pltpu.VMEM)
    return pl.pallas_call(
        place_kernel,
        out_shape=(
            jax.ShapeDtypeStruct((2, 2, XM, SHARD), BF16),
            jax.ShapeDtypeStruct((2, 2, 32, XM), BF16),
        ),
        in_specs=[hbm, hbm, hbm, vmem, vmem],
        out_specs=(hbm, hbm),
        scratch_shapes=[
            pltpu.SMEM((1, 2), I32),
            pltpu.SMEM((2,), I32),
            pltpu.SMEM((2,), I32),
            pltpu.VMEM((2, 2, XM, SHARD), BF16),
            pltpu.SemaphoreType.DMA((12,)),
        ],
        compiler_params=pltpu.CompilerParams(vmem_limit_bytes=16 << 20),
        name="place",
    )(offsets, column_index, subgrid_offsets, gathered, grids)


def per_device(facet_spectra, facet_offsets, column_index, subgrid_offsets, weights):
    spectra = facet_spectra.reshape(2, 2, XM, SHARD)
    subgrid_offsets = subgrid_offsets.reshape(2)
    grids, gathered = exchange(
        facet_offsets, column_index, subgrid_offsets, spectra, weights.reshape(2, 32, XM)
    )
    updates, grids = place(facet_offsets, column_index, subgrid_offsets, gathered, grids)
    return grids.reshape(2, 1, 2, 32, XM), updates.reshape(2, 1, 2, XM, SHARD)


def solution(mesh):
    in_specs = (
        P(None, "facet", None, None, "col"),
        P("facet", None),
        P(),
        P(None, "col"),
        P(None, "col", "facet", None),
    )
    out_specs = (P(None, "col", None, "facet", None), P(None, "facet", None, None, "col"))
    return jax.shard_map(
        per_device, mesh=mesh, in_specs=in_specs, out_specs=out_specs, check_vma=False
    )
```

```python
import math

import jax
import jax.numpy as jnp
import numpy as np
from jax import lax
from jax.experimental import pallas as pl
from jax.experimental.pallas import tpu as pltpu
from jax.sharding import PartitionSpec as P

XM = 512
WM = 128
XA = 448
SHARD = 1024
HALF = WM // 2
FACETS = 16
F32 = jnp.float32
BF16 = jnp.bfloat16
I32 = jnp.int32
MESH = pl.DeviceIdType.MESH


def tables():
    place = np.arange(WM)
    cell = np.arange(XM)
    turns = (place[:, None] - WM // 2) * (cell[None, :] - XM // 2) % XM
    angle = 2.0 * math.pi * turns / XM
    relative = (place + 0.5 - WM / 2.0) / (WM / 2.0)
    taper = (0.3 + 0.7 * (1.0 - relative * relative)) / math.sqrt(WM * FACETS)
    real = (taper[:, None] * np.cos(angle)).astype(np.float32)
    imag = (taper[:, None] * np.sin(angle)).astype(np.float32)
    wide = np.concatenate([real, imag], axis=1)
    tall = np.concatenate([real.T, imag.T], axis=1)
    return wide.astype(BF16), np.ascontiguousarray(tall).astype(BF16)


def phase(turn):
    quarter = lax.shift_right_logical(turn + 8192, 14)
    angle = (turn - quarter * 16384).astype(F32) * (2.0 * math.pi / 65536.0)
    square = angle * angle
    sine = angle * (
        1.0 + square * (-1.0 / 6.0 + square * (1.0 / 120.0 + square * (-1.0 / 5040.0 + square * (1.0 / 362880.0))))
    )
    cosine = 1.0 + square * (-0.5 + square * (1.0 / 24.0 + square * (-1.0 / 720.0 + square * (1.0 / 40320.0))))
    odd = (quarter & 1) == 1
    first = jnp.where(odd, sine, cosine)
    second = jnp.where(odd, cosine, sine)
    cosine = jnp.where(((quarter + 1) & 2) == 2, -first, first)
    sine = jnp.where((quarter & 2) == 2, -second, second)
    return cosine, sine


def turns(column_pos, first, second, k):
    return (column_pos * first + 4 * (k * second)) & 65535


def iota(shape, dim):
    return lax.broadcasted_iota(I32, shape, dim)


def dot(a, b):
    return jnp.dot(a, b, preferred_element_type=F32)


def exchange_kernel(
    offs_hbm, colidx_hbm, sub_hbm, x_hbm, w_hbm, t_hbm, tt_hbm,
    grid_out, g,
    offs_ref, colidx_ref, sub_ref, x_v, w_v, t_v, tt_v, y, r1, rx, ex, s2, rz, eo,
    grid_v, local_sem, ss, rs,
):
    f = lax.axis_index("facet")
    c = lax.axis_index("col")
    core = f % 2
    x = (f // 2) % 4
    zh = f // 8
    z_lo = c % 4
    c_prev = (c + 15) % 16
    c_next = (c + 1) % 16
    zh_prev = jnp.where(z_lo == 0, 1 - zh, zh)
    zh_next = jnp.where(z_lo == 3, 1 - zh, zh)

    def facet(half, place_x, which):
        return half * 8 + place_x * 2 + which

    def x_of(d):
        return (x + d) % 4

    f_core = facet(zh, x, 1 - core)
    f_z = facet(1 - zh, x, core)
    f_x = [f] + [facet(zh, x_of(d), core) for d in (1, 2, 3)]

    barrier = pltpu.get_barrier_semaphore()
    peers = [(f_core, c), (f_z, c), (f_x[1], c), (f_x[2], c), (f_x[3], c)]
    peers += [(facet(zh_prev, x_of(d), core), c_prev) for d in range(4)]
    peers += [(facet(zh_next, x_of(d), core), c_next) for d in range(4)]
    for peer in peers:
        pl.semaphore_signal(barrier, inc=1, device_id=peer, device_id_type=MESH)

    loads = [
        pltpu.make_async_copy(t_hbm, t_v, local_sem.at[2]),
        pltpu.make_async_copy(tt_hbm, tt_v, local_sem.at[3]),
        pltpu.make_async_copy(w_hbm, w_v.at[zh], local_sem.at[4]),
    ]
    spectra = [
        [
            pltpu.make_async_copy(
                x_hbm.at[col, part, pl.ds(256 * half, 256)],
                x_v.at[col, part, pl.ds(256 * half, 256)],
                local_sem.at[col],
            )
            for half in range(2) for part in range(2)
        ]
        for col in range(2)
    ]
    scalars = [
        pltpu.make_async_copy(source, target, local_sem.at[6 + index])
        for index, (source, target) in enumerate(
            ((offs_hbm, offs_ref), (colidx_hbm, colidx_ref), (sub_hbm, sub_ref))
        )
    ]
    for load in scalars:
        load.start()
    for load in spectra[0]:
        load.start()

    used = []

    def group():
        used.append(None)
        return rs.at[len(used) - 1]

    sent = []

    def send(src, dst, arrived, f_to, c_to=None):
        sent.append(math.prod(src.shape))
        pltpu.make_async_remote_copy(
            src_ref=src, dst_ref=dst, send_sem=ss.at[0], recv_sem=arrived,
            device_id=(f_to, c if c_to is None else c_to), device_id_type=MESH,
        ).start()

    def arrive(whole, arrived):
        pltpu.make_async_copy(whole, whole, arrived).wait()

    for load in scalars:
        load.wait()
    for load in spectra[1]:
        load.start()
    lane = iota((16, 128), 1)
    first, second = offs_ref[0, 0], offs_ref[0, 1]
    starts = []
    for col in range(2):
        starts.append(lax.shift_right_arithmetic(sub_ref[col], 2) - c * SHARD - HALF)

    def phased(col):
        start = starts[col]
        column_pos = colidx_ref[col] * XA
        cosine, sine = phase(turns(column_pos, first, second, c * SHARD + start + iota((8, 128), 1)))
        cosine, sine = cosine[0:1], sine[0:1]
        spot = iota((8, 128), 1)
        spot = c * SHARD + jnp.where(spot < HALF, spot, SHARD - 128 + spot)
        cosine_e, sine_e = phase(turns(column_pos, first, second, spot))
        cosine_e, sine_e = cosine_e[0:1], sine_e[0:1]
        tile = jnp.clip(lax.shift_right_arithmetic(start, 7), 0, SHARD // 128 - 2)
        pick = (iota((256, 128), 0) + tile * 128 == iota((256, 128), 1) + start).astype(F32).astype(BF16)
        bits = [(jnp.full((128, 128), 0, I32) + tile) & (1 << bit) != 0 for bit in range(3)]
        wide = iota((128, 128), 1) < HALF

        for q in range(4):
            span = pl.ds(q * 128, 128)
            pairs = []
            for part in range(2):
                tiles = [x_v[col, part, span, 128 * i:128 * i + 128] for i in range(8)]
                for bit, width in ((2, 5), (1, 3), (0, 2)):
                    far = 1 << bit
                    tiles = [
                        jnp.where(bits[bit], tiles[i + far], tiles[i]) if i + far < len(tiles) else tiles[i]
                        for i in range(width)
                    ]
                pairs.append(jnp.concatenate(tiles, axis=1))
            main_re = dot(pairs[0], pick)
            main_im = dot(pairs[1], pick)
            out_re = (main_re * cosine + main_im * sine).astype(BF16)
            out_im = (main_im * cosine - main_re * sine).astype(BF16)
            edge_re = jnp.where(wide, x_v[col, 0, span, 0:128].astype(F32), x_v[col, 0, span, SHARD - 128:SHARD].astype(F32))
            edge_im = jnp.where(wide, x_v[col, 1, span, 0:128].astype(F32), x_v[col, 1, span, SHARD - 128:SHARD].astype(F32))
            e_re = edge_re * cosine_e + edge_im * sine_e
            e_im = edge_im * cosine_e - edge_re * sine_e
            swap_re = pltpu.roll(e_re, 64, 1)
            swap_im = pltpu.roll(e_im, 64, 1)
            for j in range(4):
                xx, cc = (q % 2) * 2 + j // 2, j % 2
                block = y.at[col, cc, xx, q // 2]
                a, b, d = 32 * j, 32 * j + 16, 32 * j + 32
                block[0:32] = out_re[a:d]
                block[32:64] = out_im[a:d]
                block[64:80] = jnp.where(lane < HALF, e_re[a:b], swap_re[b:d]).astype(BF16)
                block[80:96] = jnp.where(lane < HALF, e_im[a:b], swap_im[b:d]).astype(BF16)
                block[96:112] = jnp.where(lane < HALF, swap_re[a:b], e_re[b:d]).astype(BF16)
                block[112:128] = jnp.where(lane < HALF, swap_im[a:b], e_im[b:d]).astype(BF16)

    def total(*refs):
        result = refs[0][...].astype(F32)
        for ref in refs[1:]:
            result = result + ref[...].astype(F32)
        return result

    order = (2, 1, 3, 0)
    from_core = [group() for _ in range(2)]
    from_z_weights = group()
    for col in range(2):
        arrive(x_v.at[col], local_sem.at[col])
        if col == 1:
            for load in loads:
                load.start()
        phased(col)
        if col == 0:
            pl.semaphore_wait(barrier, len(peers))
        send(y.at[col, 1 - core], r1.at[col], from_core[col], f_core)
    send(w_hbm, w_v.at[zh], from_z_weights, f_z)

    from_x = [group() for _ in range(2)]
    from_near = [group() for _ in range(2)]
    for col in range(2):
        arrive(r1.at[col], from_core[col])
        for d in order:
            xx = x_of(d)
            y[col, core, xx] = total(y.at[col, core, xx], r1.at[col, xx]).astype(BF16)
            block = y.at[col, core, xx]
            send(block.at[:, pl.ds(64, 32)], ex.at[col, 1, d], from_near[col], facet(zh_prev, xx, core), c_prev)
            send(block.at[:, pl.ds(96, 32)], ex.at[col, 0, d], from_near[col], facet(zh_next, xx, core), c_next)
            if d:
                send(block.at[:, pl.ds(0, 64)], rx.at[col, d - 1], from_x[col], f_x[d])

    def matrix(source, window, start):
        cell = (source & 63) + jnp.where(source < 128, -HALF, SHARD) - start
        same = (lax.shift_right_logical(source, 6) & 1) == lax.shift_right_logical(window, 7)
        return jnp.where(same & (cell == (window & 127)), 1.0, 0.0).astype(BF16)

    side0, side1 = iota((256, 256), 0), iota((256, 256), 1)
    gather_in = [matrix(side0, side1, start) for start in starts]
    gather_out = [matrix(side1, side0, start) for start in starts]

    from_z = [group() for _ in range(2)]
    for col in range(2):
        arrive(rx.at[col], from_x[col])
        main = total(y.at[col, core, x, :, pl.ds(0, 64)], rx.at[col, 0], rx.at[col, 1], rx.at[col, 2])
        arrive(ex.at[col], from_near[col])
        low, high = (total(*(ex.at[col, side, d] for d in range(4))).reshape(64, 128) for side in range(2))
        edge = dot(jnp.concatenate([low, high], axis=1).astype(BF16), gather_in[col])
        for half in range(2):
            for part in range(2):
                a = half * 32 + part * 16
                reach = jnp.concatenate([edge[a:a + 16, 0:128], edge[a:a + 16, 128:256]], axis=0)
                rows = slice(part * 32, part * 32 + 32)
                s2[col, half, rows] = (main[half, rows] + reach).astype(BF16)
        send(s2.at[col], rz.at[col], from_z[col], f_z)

    for load in loads:
        load.wait()
    arrive(w_v.at[1 - zh], from_z_weights)

    from_mains = [[group() for _ in range(3)] for _ in range(2)]
    from_edges = [[group() for _ in range(4)] for _ in range(2)]
    passed = [[group() for _ in range(2)] for _ in range(2)]
    for col in range(2):
        arrive(rz.at[col], from_z[col])
        main = total(s2.at[col], rz.at[col])
        window = jnp.concatenate(
            [main[half, part * 32:part * 32 + 32] for part in range(2) for half in range(2)], axis=0
        ).astype(BF16)
        prod = dot(window, t_v[...])
        cells_re = (prod[0:64, 0:XM] - prod[64:128, XM:2 * XM]).astype(BF16)
        cells_im = (prod[0:64, XM:2 * XM] + prod[64:128, 0:XM]).astype(BF16)
        weight = jnp.concatenate([w_v[0, col], w_v[1, col]], axis=0).astype(F32)
        scaled_re = (cells_re.astype(F32) * weight).astype(BF16)
        scaled_im = (cells_im.astype(F32) * weight).astype(BF16)
        prod = dot(jnp.concatenate([scaled_re, scaled_im], axis=0), tt_v[...])
        back_re = (prod[0:64, 0:WM] + prod[64:128, WM:2 * WM]).astype(BF16)
        back_im = (prod[64:128, 0:WM] - prod[0:64, WM:2 * WM]).astype(BF16)
        for half in range(2):
            grid_v[half, col, 0] = cells_re[half * 32:half * 32 + 32]
            grid_v[half, col, 1] = cells_im[half * 32:half * 32 + 32]
        packed = []
        for half in range(2):
            block = g.at[col, half, x, core]
            a = half * 32
            block[0:32] = back_re[a:a + 32]
            block[32:64] = back_im[a:a + 32]
            for back in (back_re, back_im):
                packed.append(jnp.concatenate([back[a:a + 16], back[a + 16:a + 32]], axis=1))
        out_edge = dot(jnp.concatenate(packed, axis=0), gather_out[col]).astype(BF16)
        eo[col, 0] = out_edge[:, 0:128].reshape(2, 32, 128)
        eo[col, 1] = out_edge[:, 128:256].reshape(2, 32, 128)
        low, high = g.at[col, :, x, core, pl.ds(64, 32)], g.at[col, :, x, core, pl.ds(96, 32)]
        for d in order:
            send(eo.at[col, 0], high, from_edges[col][d], facet(zh_prev, x_of(d), core), c_prev)
            send(eo.at[col, 1], low, from_edges[col][d], facet(zh_next, x_of(d), core), c_next)
        home = g.at[col, :, x, core, pl.ds(0, 64)]
        for d in (2, 1, 3):
            send(home, home, from_mains[col][d - 1], f_x[d])
        send(home, home, passed[col][0], f_core)

    grid_copy = pltpu.make_async_copy(grid_v.at[zh], grid_out, local_sem.at[5])
    grid_copy.start()

    for col in range(2):
        for d in (1, 3, 2):
            block = g.at[col, :, x_of(4 - d), core, pl.ds(0, 64)]
            arrive(block, from_mains[col][d - 1])
            send(block, block, passed[col][0], f_core)
        for d in order:
            block = g.at[col, :, x_of(4 - d), core, pl.ds(64, 64)]
            arrive(block, from_edges[col][d])
            send(block, block, passed[col][1], f_core)
    for col in range(2):
        for half in range(2):
            arrive(g.at[col, :, :, 1 - core, pl.ds(64 * half, 64)], passed[col][half])

    assert len(used) == N_GROUPS
    every = sum(sent) // SHARD
    arrive(x_v.reshape(2 * 2 * XM, SHARD).at[pl.ds(0, every)], ss.at[0])
    grid_copy.wait()


N_GROUPS = 27


def exchange(offsets, column_index, subgrid_offsets, spectra, weights):
    table, table_t = tables()
    hbm = pl.BlockSpec(memory_space=pltpu.HBM)
    vmem = pl.BlockSpec(memory_space=pltpu.VMEM)
    return pl.pallas_call(
        exchange_kernel,
        out_shape=(
            pltpu.VMEM((2, 2, 32, XM), BF16),
            pltpu.VMEM((2, 2, 4, 2, 128, 128), BF16),
        ),
        in_specs=[hbm] * 7,
        out_specs=(vmem, vmem),
        scratch_shapes=[
            pltpu.SMEM((1, 2), I32),
            pltpu.SMEM((2,), I32),
            pltpu.SMEM((2,), I32),
            pltpu.VMEM((2, 2, XM, SHARD), BF16),
            pltpu.VMEM((2, 2, 32, XM), BF16),
            pltpu.VMEM((WM, 2 * XM), BF16),
            pltpu.VMEM((XM, 2 * WM), BF16),
            pltpu.VMEM((2, 2, 4, 2, 128, 128), BF16),
            pltpu.VMEM((2, 4, 2, 128, 128), BF16),
            pltpu.VMEM((2, 3, 2, 64, 128), BF16),
            pltpu.VMEM((2, 2, 4, 2, 32, 128), BF16),
            pltpu.VMEM((2, 2, 64, 128), BF16),
            pltpu.VMEM((2, 2, 64, 128), BF16),
            pltpu.VMEM((2, 2, 2, 32, 128), BF16),
            pltpu.VMEM((2, 2, 2, 32, XM), BF16),
            pltpu.SemaphoreType.DMA((9,)),
            pltpu.SemaphoreType.DMA((1,)),
            pltpu.SemaphoreType.DMA((N_GROUPS,)),
        ],
        compiler_params=pltpu.CompilerParams(collective_id=0, has_side_effects=True),
        name="exchange",
    )(offsets, column_index, subgrid_offsets, spectra, weights, jnp.asarray(table), jnp.asarray(table_t))


def place_kernel(offs_hbm, colidx_hbm, sub_hbm, u_ref, grid_ref, out_hbm, grid_hbm, offs_ref, colidx_ref, sub_ref, out, sem):
    grid_copy = pltpu.make_async_copy(grid_ref, grid_hbm, sem.at[0])
    grid_copy.start()
    scalars = [
        pltpu.make_async_copy(source, target, sem.at[9 + index])
        for index, (source, target) in enumerate(
            ((offs_hbm, offs_ref), (colidx_hbm, colidx_ref), (sub_hbm, sub_ref))
        )
    ]
    for load in scalars:
        load.start()
    for col in range(2):
        out[col] = jnp.zeros((2, XM, SHARD), BF16)
    for load in scalars:
        load.wait()
    c = lax.axis_index("col")
    first, second = offs_ref[0, 0], offs_ref[0, 1]
    spot = iota((8, 128), 1)
    spot = c * SHARD + jnp.where(spot < HALF, spot, SHARD - 128 + spot)
    lane = iota((16, 128), 1)
    wide = iota((32, 128), 1) < HALF
    for col in range(2):
        start = lax.shift_right_arithmetic(sub_ref[col], 2) - c * SHARD - HALF
        base = jnp.clip(lax.shift_right_arithmetic(start, 7), 0, SHARD // 128 - 2) * 128
        column_pos = colidx_ref[col] * XA
        cosine, sine = phase(turns(column_pos, first, second, c * SHARD + base + iota((8, 256), 1)))
        cosine, sine = cosine[0:1], sine[0:1]
        cosine_e, sine_e = phase(turns(column_pos, first, second, spot))
        cosine_e, sine_e = cosine_e[0:1], sine_e[0:1]
        put = (iota((128, 256), 1) + base == iota((128, 256), 0) + start).astype(F32).astype(BF16)
        tiles = pl.ds(pl.multiple_of(base, 128), 256)

        for q in range(4):
            span = pl.ds(q * 128, 128)
            some = u_ref.at[col, q // 2, pl.ds((q % 2) * 2, 2)]
            moved = dot(some[:, :, 0:64].reshape(256, 128), put)
            for j in range(4):
                block = some.at[j // 2, j % 2]
                rows = pl.ds(q * 128 + 32 * j, 32)
                low_re, low_im = block[64:80].astype(F32), block[80:96].astype(F32)
                top_re, top_im = block[96:112].astype(F32), block[112:128].astype(F32)
                edges = []
                for low, top in ((low_re, top_re), (low_im, top_im)):
                    edges.append(jnp.concatenate([
                        jnp.where(lane < HALF, low, pltpu.roll(top, 64, 1)),
                        jnp.where(lane < HALF, pltpu.roll(low, 64, 1), top),
                    ], axis=0))
                edge_re = edges[0] * cosine_e - edges[1] * sine_e
                edge_im = edges[1] * cosine_e + edges[0] * sine_e
                zero = jnp.zeros_like(edge_re)
                for part, edge in ((0, edge_re), (1, edge_im)):
                    out[col, part, rows, 0:128] = jnp.where(wide, edge, zero).astype(BF16)
                    out[col, part, rows, SHARD - 128:SHARD] = jnp.where(wide, zero, edge).astype(BF16)
                main_re, main_im = moved[64 * j:64 * j + 32], moved[64 * j + 32:64 * j + 64]
                out_re = main_re * cosine - main_im * sine
                out_im = main_im * cosine + main_re * sine
                for part, value in ((0, out_re), (1, out_im)):
                    out[col, part, rows, tiles] = (out[col, part, rows, tiles].astype(F32) + value).astype(BF16)
            pltpu.make_async_copy(out.at[col, :, span], out_hbm.at[col, :, span], sem.at[1 + col * 4 + q]).start()

    for col in range(2):
        for q in range(4):
            span = pl.ds(q * 128, 128)
            pltpu.make_async_copy(out.at[col, :, span], out_hbm.at[col, :, span], sem.at[1 + col * 4 + q]).wait()
    grid_copy.wait()


def place(offsets, column_index, subgrid_offsets, gathered, grids):
    hbm = pl.BlockSpec(memory_space=pltpu.HBM)
    vmem = pl.BlockSpec(memory_space=pltpu.VMEM)
    gathered = pltpu.with_memory_space_constraint(gathered, pltpu.VMEM)
    grids = pltpu.with_memory_space_constraint(grids, pltpu.VMEM)
    return pl.pallas_call(
        place_kernel,
        out_shape=(
            jax.ShapeDtypeStruct((2, 2, XM, SHARD), BF16),
            jax.ShapeDtypeStruct((2, 2, 32, XM), BF16),
        ),
        in_specs=[hbm, hbm, hbm, vmem, vmem],
        out_specs=(hbm, hbm),
        scratch_shapes=[
            pltpu.SMEM((1, 2), I32),
            pltpu.SMEM((2,), I32),
            pltpu.SMEM((2,), I32),
            pltpu.VMEM((2, 2, XM, SHARD), BF16),
            pltpu.SemaphoreType.DMA((12,)),
        ],
        compiler_params=pltpu.CompilerParams(vmem_limit_bytes=16 << 20),
        name="place",
    )(offsets, column_index, subgrid_offsets, gathered, grids)


def per_device(facet_spectra, facet_offsets, column_index, subgrid_offsets, weights):
    spectra = facet_spectra.reshape(2, 2, XM, SHARD)
    subgrid_offsets = subgrid_offsets.reshape(2)
    grids, gathered = exchange(
        facet_offsets, column_index, subgrid_offsets, spectra, weights.reshape(2, 32, XM)
    )
    updates, grids = place(facet_offsets, column_index, subgrid_offsets, gathered, grids)
    return grids.reshape(2, 1, 2, 32, XM), updates.reshape(2, 1, 2, XM, SHARD)


def solution(mesh):
    in_specs = (
        P(None, "facet", None, None, "col"),
        P("facet", None),
        P(),
        P(None, "col"),
        P(None, "col", "facet", None),
    )
    out_specs = (P(None, "col", None, "facet", None), P(None, "facet", None, None, "col"))
    return jax.shard_map(
        per_device, mesh=mesh, in_specs=in_specs, out_specs=out_specs, check_vma=False
    )
```

```python
import math

import jax
import jax.numpy as jnp
import numpy as np
from jax import lax
from jax.experimental import pallas as pl
from jax.experimental.pallas import tpu as pltpu
from jax.sharding import PartitionSpec as P

XM = 512
WM = 128
XA = 448
SHARD = 1024
HALF = WM // 2
FACETS = 16
F32 = jnp.float32
BF16 = jnp.bfloat16
I32 = jnp.int32
MESH = pl.DeviceIdType.MESH


def tables():
    place = np.arange(WM)
    cell = np.arange(XM)
    turns = (place[:, None] - WM // 2) * (cell[None, :] - XM // 2) % XM
    angle = 2.0 * math.pi * turns / XM
    relative = (place + 0.5 - WM / 2.0) / (WM / 2.0)
    taper = (0.3 + 0.7 * (1.0 - relative * relative)) / math.sqrt(WM * FACETS)
    real = (taper[:, None] * np.cos(angle)).astype(np.float32)
    imag = (taper[:, None] * np.sin(angle)).astype(np.float32)
    wide = np.concatenate([real, imag], axis=1)
    tall = np.concatenate([real.T, imag.T], axis=1)
    return wide.astype(BF16), np.ascontiguousarray(tall).astype(BF16)


def phase(turn):
    quarter = lax.shift_right_logical(turn + 8192, 14)
    angle = (turn - quarter * 16384).astype(F32) * (2.0 * math.pi / 65536.0)
    square = angle * angle
    sine = angle * (
        1.0 + square * (-1.0 / 6.0 + square * (1.0 / 120.0 + square * (-1.0 / 5040.0 + square * (1.0 / 362880.0))))
    )
    cosine = 1.0 + square * (-0.5 + square * (1.0 / 24.0 + square * (-1.0 / 720.0 + square * (1.0 / 40320.0))))
    odd = (quarter & 1) == 1
    first = jnp.where(odd, sine, cosine)
    second = jnp.where(odd, cosine, sine)
    cosine = jnp.where(((quarter + 1) & 2) == 2, -first, first)
    sine = jnp.where((quarter & 2) == 2, -second, second)
    return cosine, sine


def turns(column_pos, first, second, k):
    return (column_pos * first + 4 * (k * second)) & 65535


def iota(shape, dim):
    return lax.broadcasted_iota(I32, shape, dim)


def dot(a, b):
    return jnp.dot(a, b, preferred_element_type=F32)


def exchange_kernel(
    offs_hbm, colidx_hbm, sub_hbm, x_hbm, w_hbm, t_hbm, tt_hbm,
    grid_out, g, info,
    offs_ref, colidx_ref, sub_ref, x_v, w_v, t_v, tt_v, y, r1, rx, ex, s2, rz, eo,
    grid_v, local_sem, ss, rs,
):
    f = lax.axis_index("facet")
    c = lax.axis_index("col")
    core = f % 2
    x = (f // 2) % 4
    zh = f // 8
    z_lo = c % 4
    c_prev = (c + 15) % 16
    c_next = (c + 1) % 16
    zh_prev = jnp.where(z_lo == 0, 1 - zh, zh)
    zh_next = jnp.where(z_lo == 3, 1 - zh, zh)

    def facet(half, place_x, which):
        return half * 8 + place_x * 2 + which

    def x_of(d):
        return (x + d) % 4

    f_core = facet(zh, x, 1 - core)
    f_z = facet(1 - zh, x, core)
    f_x = [f] + [facet(zh, x_of(d), core) for d in (1, 2, 3)]

    barrier = pltpu.get_barrier_semaphore()
    peers = [(f_core, c), (f_z, c), (f_x[1], c), (f_x[2], c), (f_x[3], c)]
    peers += [(facet(zh_prev, x_of(d), core), c_prev) for d in range(4)]
    peers += [(facet(zh_next, x_of(d), core), c_next) for d in range(4)]
    for peer in peers:
        pl.semaphore_signal(barrier, inc=1, device_id=peer, device_id_type=MESH)

    loads = [
        pltpu.make_async_copy(t_hbm, t_v, local_sem.at[2]),
        pltpu.make_async_copy(tt_hbm, tt_v, local_sem.at[3]),
        pltpu.make_async_copy(w_hbm, w_v.at[zh], local_sem.at[4]),
    ]
    spectra = [
        [
            pltpu.make_async_copy(
                x_hbm.at[col, part, pl.ds(256 * half, 256)],
                x_v.at[col, part, pl.ds(256 * half, 256)],
                local_sem.at[col],
            )
            for half in range(2) for part in range(2)
        ]
        for col in range(2)
    ]
    scalars = [
        pltpu.make_async_copy(source, target, local_sem.at[6 + index])
        for index, (source, target) in enumerate(
            ((offs_hbm, offs_ref), (colidx_hbm, colidx_ref), (sub_hbm, sub_ref))
        )
    ]
    for load in scalars:
        load.start()
    for load in spectra[0]:
        load.start()

    used = []

    def group():
        used.append(None)
        return rs.at[len(used) - 1]

    sent = []

    def send(src, dst, arrived, f_to, c_to=None):
        sent.append(math.prod(src.shape))
        pltpu.make_async_remote_copy(
            src_ref=src, dst_ref=dst, send_sem=ss.at[0], recv_sem=arrived,
            device_id=(f_to, c if c_to is None else c_to), device_id_type=MESH,
        ).start()

    def arrive(whole, arrived):
        pltpu.make_async_copy(whole, whole, arrived).wait()

    for load in scalars:
        load.wait()
    for load in spectra[1]:
        load.start()
    lane = iota((16, 128), 1)
    first, second = offs_ref[0, 0], offs_ref[0, 1]
    starts = []
    for col in range(2):
        starts.append(lax.shift_right_arithmetic(sub_ref[col], 2) - c * SHARD - HALF)

    def prepared(col):
        start = starts[col]
        column_pos = colidx_ref[col] * XA
        cosine, sine = phase(turns(column_pos, first, second, c * SHARD + start + iota((8, 128), 1)))
        cosine, sine = cosine[0:1], sine[0:1]
        spot = iota((8, 128), 1)
        spot = c * SHARD + jnp.where(spot < HALF, spot, SHARD - 128 + spot)
        cosine_e, sine_e = phase(turns(column_pos, first, second, spot))
        cosine_e, sine_e = cosine_e[0:1], sine_e[0:1]
        tile = jnp.clip(lax.shift_right_arithmetic(start, 7), 0, SHARD // 128 - 2)
        pick = (iota((256, 128), 0) + tile * 128 == iota((256, 128), 1) + start).astype(F32).astype(BF16)
        bits = [(jnp.full((128, 128), 0, I32) + tile) & (1 << bit) != 0 for bit in range(3)]
        return cosine, sine, cosine_e, sine_e, pick, bits

    wide = iota((128, 128), 1) < HALF

    def phased(col, cosine, sine, cosine_e, sine_e, pick, bits):
        for q in range(4):
            span = pl.ds(q * 128, 128)
            pairs = []
            for part in range(2):
                tiles = [x_v[col, part, span, 128 * i:128 * i + 128] for i in range(8)]
                for bit, width in ((2, 5), (1, 3), (0, 2)):
                    far = 1 << bit
                    tiles = [
                        jnp.where(bits[bit], tiles[i + far], tiles[i]) if i + far < len(tiles) else tiles[i]
                        for i in range(width)
                    ]
                pairs.append(jnp.concatenate(tiles, axis=1))
            main_re = dot(pairs[0], pick)
            main_im = dot(pairs[1], pick)
            out_re = (main_re * cosine + main_im * sine).astype(BF16)
            out_im = (main_im * cosine - main_re * sine).astype(BF16)
            edge_re = jnp.where(wide, x_v[col, 0, span, 0:128].astype(F32), x_v[col, 0, span, SHARD - 128:SHARD].astype(F32))
            edge_im = jnp.where(wide, x_v[col, 1, span, 0:128].astype(F32), x_v[col, 1, span, SHARD - 128:SHARD].astype(F32))
            e_re = edge_re * cosine_e + edge_im * sine_e
            e_im = edge_im * cosine_e - edge_re * sine_e
            swap_re = pltpu.roll(e_re, 64, 1)
            swap_im = pltpu.roll(e_im, 64, 1)
            for j in range(4):
                xx, cc = (q % 2) * 2 + j // 2, j % 2
                block = y.at[col, cc, xx, q // 2]
                a, b, d = 32 * j, 32 * j + 16, 32 * j + 32
                block[0:32] = out_re[a:d]
                block[32:64] = out_im[a:d]
                block[64:80] = jnp.where(lane < HALF, e_re[a:b], swap_re[b:d]).astype(BF16)
                block[80:96] = jnp.where(lane < HALF, e_im[a:b], swap_im[b:d]).astype(BF16)
                block[96:112] = jnp.where(lane < HALF, swap_re[a:b], e_re[b:d]).astype(BF16)
                block[112:128] = jnp.where(lane < HALF, swap_im[a:b], e_im[b:d]).astype(BF16)

    def total(*refs):
        result = refs[0][...].astype(F32)
        for ref in refs[1:]:
            result = result + ref[...].astype(F32)
        return result

    order = (2, 1, 3, 0)
    from_core = [group() for _ in range(2)]
    from_z_weights = group()
    ready = [prepared(col) for col in range(2)]
    row = iota((8, 128), 0)
    known = [starts[0], starts[1]] + [(colidx_ref[col] * XA * first) & 65535 for col in range(2)] + [second]
    facts = jnp.zeros((8, 128), I32)
    for index, value in enumerate(known):
        facts = jnp.where(row == index, value, facts)
    info[...] = facts.astype(F32)
    for col in range(2):
        arrive(x_v.at[col], local_sem.at[col])
        if col == 1:
            for load in loads:
                load.start()
        phased(col, *ready[col])
        if col == 0:
            pl.semaphore_wait(barrier, len(peers))
        send(y.at[col, 1 - core], r1.at[col], from_core[col], f_core)
    send(w_hbm, w_v.at[zh], from_z_weights, f_z)

    from_x = [group() for _ in range(2)]
    from_near = [group() for _ in range(2)]
    for col in range(2):
        arrive(r1.at[col], from_core[col])
        for d in order:
            xx = x_of(d)
            y[col, core, xx] = total(y.at[col, core, xx], r1.at[col, xx]).astype(BF16)
            block = y.at[col, core, xx]
            send(block.at[:, pl.ds(64, 32)], ex.at[col, 1, d], from_near[col], facet(zh_prev, xx, core), c_prev)
            send(block.at[:, pl.ds(96, 32)], ex.at[col, 0, d], from_near[col], facet(zh_next, xx, core), c_next)
            if d:
                send(block.at[:, pl.ds(0, 64)], rx.at[col, d - 1], from_x[col], f_x[d])

    def matrix(source, window, start):
        cell = (source & 63) + jnp.where(source < 128, -HALF, SHARD) - start
        same = (lax.shift_right_logical(source, 6) & 1) == lax.shift_right_logical(window, 7)
        return jnp.where(same & (cell == (window & 127)), 1.0, 0.0).astype(BF16)

    side0, side1 = iota((256, 256), 0), iota((256, 256), 1)
    gather_in = [matrix(side0, side1, start) for start in starts]
    gather_out = [matrix(side1, side0, start) for start in starts]

    from_z = [group() for _ in range(2)]
    for col in range(2):
        arrive(rx.at[col], from_x[col])
        main = total(y.at[col, core, x, :, pl.ds(0, 64)], rx.at[col, 0], rx.at[col, 1], rx.at[col, 2])
        arrive(ex.at[col], from_near[col])
        low, high = (total(*(ex.at[col, side, d] for d in range(4))).reshape(64, 128) for side in range(2))
        edge = dot(jnp.concatenate([low, high], axis=1).astype(BF16), gather_in[col])
        for half in range(2):
            for part in range(2):
                a = half * 32 + part * 16
                reach = jnp.concatenate([edge[a:a + 16, 0:128], edge[a:a + 16, 128:256]], axis=0)
                rows = slice(part * 32, part * 32 + 32)
                s2[col, half, rows] = (main[half, rows] + reach).astype(BF16)
        send(s2.at[col], rz.at[col], from_z[col], f_z)

    for load in loads:
        load.wait()
    arrive(w_v.at[1 - zh], from_z_weights)

    from_mains = [[group() for _ in range(3)] for _ in range(2)]
    from_edges = [[group() for _ in range(4)] for _ in range(2)]
    passed = [[group() for _ in range(2)] for _ in range(2)]
    for col in range(2):
        arrive(rz.at[col], from_z[col])
        main = total(s2.at[col], rz.at[col])
        window = jnp.concatenate(
            [main[half, part * 32:part * 32 + 32] for part in range(2) for half in range(2)], axis=0
        ).astype(BF16)
        prod = dot(window, t_v[...])
        cells_re = (prod[0:64, 0:XM] - prod[64:128, XM:2 * XM]).astype(BF16)
        cells_im = (prod[0:64, XM:2 * XM] + prod[64:128, 0:XM]).astype(BF16)
        weight = jnp.concatenate([w_v[0, col], w_v[1, col]], axis=0).astype(F32)
        scaled_re = (cells_re.astype(F32) * weight).astype(BF16)
        scaled_im = (cells_im.astype(F32) * weight).astype(BF16)
        prod = dot(jnp.concatenate([scaled_re, scaled_im], axis=0), tt_v[...])
        back_re = (prod[0:64, 0:WM] + prod[64:128, WM:2 * WM]).astype(BF16)
        back_im = (prod[64:128, 0:WM] - prod[0:64, WM:2 * WM]).astype(BF16)
        packed = []
        for half in range(2):
            block = g.at[col, half, x, core]
            a = half * 32
            block[0:32] = back_re[a:a + 32]
            block[32:64] = back_im[a:a + 32]
            for back in (back_re, back_im):
                packed.append(jnp.concatenate([back[a:a + 16], back[a + 16:a + 32]], axis=1))
        home = g.at[col, :, x, core, pl.ds(0, 64)]
        for d in (2, 1, 3):
            send(home, home, from_mains[col][d - 1], f_x[d])
        send(home, home, passed[col][0], f_core)
        out_edge = dot(jnp.concatenate(packed, axis=0), gather_out[col]).astype(BF16)
        eo[col, 0] = out_edge[:, 0:128].reshape(2, 32, 128)
        eo[col, 1] = out_edge[:, 128:256].reshape(2, 32, 128)
        low, high = g.at[col, :, x, core, pl.ds(64, 32)], g.at[col, :, x, core, pl.ds(96, 32)]
        for d in order:
            send(eo.at[col, 0], high, from_edges[col][d], facet(zh_prev, x_of(d), core), c_prev)
            send(eo.at[col, 1], low, from_edges[col][d], facet(zh_next, x_of(d), core), c_next)
        for half in range(2):
            grid_v[half, col, 0] = cells_re[half * 32:half * 32 + 32]
            grid_v[half, col, 1] = cells_im[half * 32:half * 32 + 32]

    for col in range(2):
        for d in (1, 3, 2):
            block = g.at[col, :, x_of(4 - d), core, pl.ds(0, 64)]
            arrive(block, from_mains[col][d - 1])
            send(block, block, passed[col][0], f_core)
        for d in order:
            block = g.at[col, :, x_of(4 - d), core, pl.ds(64, 64)]
            arrive(block, from_edges[col][d])
            send(block, block, passed[col][1], f_core)
    grid_copy = pltpu.make_async_copy(grid_v.at[zh], grid_out, local_sem.at[5])
    grid_copy.start()
    for col in range(2):
        for half in range(2):
            arrive(g.at[col, :, :, 1 - core, pl.ds(64 * half, 64)], passed[col][half])

    assert len(used) == N_GROUPS
    every = sum(sent) // SHARD
    arrive(x_v.reshape(2 * 2 * XM, SHARD).at[pl.ds(0, every)], ss.at[0])
    grid_copy.wait()


N_GROUPS = 27


def exchange(offsets, column_index, subgrid_offsets, spectra, weights):
    table, table_t = tables()
    hbm = pl.BlockSpec(memory_space=pltpu.HBM)
    vmem = pl.BlockSpec(memory_space=pltpu.VMEM)
    return pl.pallas_call(
        exchange_kernel,
        out_shape=(
            pltpu.VMEM((2, 2, 32, XM), BF16),
            pltpu.VMEM((2, 2, 4, 2, 128, 128), BF16),
            pltpu.VMEM((8, 128), F32),
        ),
        in_specs=[hbm] * 7,
        out_specs=(vmem, vmem, vmem),
        scratch_shapes=[
            pltpu.SMEM((1, 2), I32),
            pltpu.SMEM((2,), I32),
            pltpu.SMEM((2,), I32),
            pltpu.VMEM((2, 2, XM, SHARD), BF16),
            pltpu.VMEM((2, 2, 32, XM), BF16),
            pltpu.VMEM((WM, 2 * XM), BF16),
            pltpu.VMEM((XM, 2 * WM), BF16),
            pltpu.VMEM((2, 2, 4, 2, 128, 128), BF16),
            pltpu.VMEM((2, 4, 2, 128, 128), BF16),
            pltpu.VMEM((2, 3, 2, 64, 128), BF16),
            pltpu.VMEM((2, 2, 4, 2, 32, 128), BF16),
            pltpu.VMEM((2, 2, 64, 128), BF16),
            pltpu.VMEM((2, 2, 64, 128), BF16),
            pltpu.VMEM((2, 2, 2, 32, 128), BF16),
            pltpu.VMEM((2, 2, 2, 32, XM), BF16),
            pltpu.SemaphoreType.DMA((9,)),
            pltpu.SemaphoreType.DMA((1,)),
            pltpu.SemaphoreType.DMA((N_GROUPS,)),
        ],
        compiler_params=pltpu.CompilerParams(collective_id=0, has_side_effects=True),
        name="exchange",
    )(offsets, column_index, subgrid_offsets, spectra, weights, jnp.asarray(table), jnp.asarray(table_t))


def place_kernel(u_ref, grid_ref, info_ref, out_hbm, grid_hbm, out, sem):
    grid_copy = pltpu.make_async_copy(grid_ref, grid_hbm, sem.at[0])
    grid_copy.start()
    known = [jnp.max(info_ref[index:index + 1, :]).astype(I32) for index in range(5)]
    c = lax.axis_index("col")
    second = known[4]
    spot = iota((8, 128), 1)
    spot = c * SHARD + jnp.where(spot < HALF, spot, SHARD - 128 + spot)
    lane = iota((16, 128), 1)
    wide = iota((32, 128), 1) < HALF
    for col in range(2):
        start = known[col]
        base = jnp.clip(lax.shift_right_arithmetic(start, 7), 0, SHARD // 128 - 2) * 128
        cosine, sine = phase(turns(known[2 + col], 1, second, c * SHARD + base + iota((8, 256), 1)))
        cosine, sine = cosine[0:1], sine[0:1]
        cosine_e, sine_e = phase(turns(known[2 + col], 1, second, spot))
        cosine_e, sine_e = cosine_e[0:1], sine_e[0:1]
        put = (iota((128, 256), 1) + base == iota((128, 256), 0) + start).astype(F32).astype(BF16)
        tiles = pl.ds(pl.multiple_of(base, 128), 256)

        for q in range(4):
            span = pl.ds(q * 128, 128)
            out[col, :, span] = jnp.zeros((2, 128, SHARD), BF16)
            some = u_ref.at[col, q // 2, pl.ds((q % 2) * 2, 2)]
            moved = dot(some[:, :, 0:64].reshape(256, 128), put)
            for j in range(4):
                block = some.at[j // 2, j % 2]
                rows = pl.ds(q * 128 + 32 * j, 32)
                low_re, low_im = block[64:80].astype(F32), block[80:96].astype(F32)
                top_re, top_im = block[96:112].astype(F32), block[112:128].astype(F32)
                edges = []
                for low, top in ((low_re, top_re), (low_im, top_im)):
                    edges.append(jnp.concatenate([
                        jnp.where(lane < HALF, low, pltpu.roll(top, 64, 1)),
                        jnp.where(lane < HALF, pltpu.roll(low, 64, 1), top),
                    ], axis=0))
                edge_re = edges[0] * cosine_e - edges[1] * sine_e
                edge_im = edges[1] * cosine_e + edges[0] * sine_e
                zero = jnp.zeros_like(edge_re)
                for part, edge in ((0, edge_re), (1, edge_im)):
                    out[col, part, rows, 0:128] = jnp.where(wide, edge, zero).astype(BF16)
                    out[col, part, rows, SHARD - 128:SHARD] = jnp.where(wide, zero, edge).astype(BF16)
                main_re, main_im = moved[64 * j:64 * j + 32], moved[64 * j + 32:64 * j + 64]
                out_re = main_re * cosine - main_im * sine
                out_im = main_im * cosine + main_re * sine
                for part, value in ((0, out_re), (1, out_im)):
                    out[col, part, rows, tiles] = (out[col, part, rows, tiles].astype(F32) + value).astype(BF16)
            pltpu.make_async_copy(out.at[col, :, span], out_hbm.at[col, :, span], sem.at[1 + col * 4 + q]).start()

    for col in range(2):
        for q in range(4):
            span = pl.ds(q * 128, 128)
            pltpu.make_async_copy(out.at[col, :, span], out_hbm.at[col, :, span], sem.at[1 + col * 4 + q]).wait()
    grid_copy.wait()


def place(gathered, grids, info):
    hbm = pl.BlockSpec(memory_space=pltpu.HBM)
    vmem = pl.BlockSpec(memory_space=pltpu.VMEM)
    gathered = pltpu.with_memory_space_constraint(gathered, pltpu.VMEM)
    grids = pltpu.with_memory_space_constraint(grids, pltpu.VMEM)
    info = pltpu.with_memory_space_constraint(info, pltpu.VMEM)
    return pl.pallas_call(
        place_kernel,
        out_shape=(
            jax.ShapeDtypeStruct((2, 2, XM, SHARD), BF16),
            jax.ShapeDtypeStruct((2, 2, 32, XM), BF16),
        ),
        in_specs=[vmem, vmem, vmem],
        out_specs=(hbm, hbm),
        scratch_shapes=[
            pltpu.VMEM((2, 2, XM, SHARD), BF16),
            pltpu.SemaphoreType.DMA((9,)),
        ],
        compiler_params=pltpu.CompilerParams(vmem_limit_bytes=16 << 20),
        name="place",
    )(gathered, grids, info)


def per_device(facet_spectra, facet_offsets, column_index, subgrid_offsets, weights):
    spectra = facet_spectra.reshape(2, 2, XM, SHARD)
    subgrid_offsets = subgrid_offsets.reshape(2)
    grids, gathered, info = exchange(
        facet_offsets, column_index, subgrid_offsets, spectra, weights.reshape(2, 32, XM)
    )
    updates, grids = place(gathered, grids, info)
    return grids.reshape(2, 1, 2, 32, XM), updates.reshape(2, 1, 2, XM, SHARD)


def solution(mesh):
    in_specs = (
        P(None, "facet", None, None, "col"),
        P("facet", None),
        P(),
        P(None, "col"),
        P(None, "col", "facet", None),
    )
    out_specs = (P(None, "col", None, "facet", None), P(None, "facet", None, None, "col"))
    return jax.shard_map(
        per_device, mesh=mesh, in_specs=in_specs, out_specs=out_specs, check_vma=False
    )
```

```python
import math

import jax
import jax.numpy as jnp
import numpy as np
from jax import lax
from jax.experimental import pallas as pl
from jax.experimental.pallas import tpu as pltpu
from jax.sharding import PartitionSpec as P

XM = 512
WM = 128
XA = 448
SHARD = 1024
HALF = WM // 2
FACETS = 16
F32 = jnp.float32
BF16 = jnp.bfloat16
I32 = jnp.int32
MESH = pl.DeviceIdType.MESH


def tables():
    place = np.arange(WM)
    cell = np.arange(XM)
    turns = (place[:, None] - WM // 2) * (cell[None, :] - XM // 2) % XM
    angle = 2.0 * math.pi * turns / XM
    relative = (place + 0.5 - WM / 2.0) / (WM / 2.0)
    taper = (0.3 + 0.7 * (1.0 - relative * relative)) / math.sqrt(WM * FACETS)
    real = (taper[:, None] * np.cos(angle)).astype(np.float32)
    imag = (taper[:, None] * np.sin(angle)).astype(np.float32)
    wide = np.concatenate([real, imag], axis=1)
    tall = np.concatenate([real.T, imag.T], axis=1)
    return wide.astype(BF16), np.ascontiguousarray(tall).astype(BF16)


def phase(turn):
    quarter = lax.shift_right_logical(turn + 8192, 14)
    angle = (turn - quarter * 16384).astype(F32) * (2.0 * math.pi / 65536.0)
    square = angle * angle
    sine = angle * (
        1.0 + square * (-1.0 / 6.0 + square * (1.0 / 120.0 + square * (-1.0 / 5040.0 + square * (1.0 / 362880.0))))
    )
    cosine = 1.0 + square * (-0.5 + square * (1.0 / 24.0 + square * (-1.0 / 720.0 + square * (1.0 / 40320.0))))
    odd = (quarter & 1) == 1
    first = jnp.where(odd, sine, cosine)
    second = jnp.where(odd, cosine, sine)
    cosine = jnp.where(((quarter + 1) & 2) == 2, -first, first)
    sine = jnp.where((quarter & 2) == 2, -second, second)
    return cosine, sine


def turns(column_pos, first, second, k):
    return (column_pos * first + 4 * (k * second)) & 65535


def iota(shape, dim):
    return lax.broadcasted_iota(I32, shape, dim)


def dot(a, b):
    return jnp.dot(a, b, preferred_element_type=F32)


def exchange_kernel(
    offs_hbm, colidx_hbm, sub_hbm, x_hbm, w_hbm, t_hbm, tt_hbm,
    grid_out, g, info,
    offs_ref, colidx_ref, sub_ref, x_v, w_v, t_v, tt_v, y, r1, rx, ex, s2, rz, eo,
    grid_v, local_sem, ss, rs,
):
    f = lax.axis_index("facet")
    c = lax.axis_index("col")
    core = f % 2
    x = (f // 2) % 4
    zh = f // 8
    z_lo = c % 4
    c_prev = (c + 15) % 16
    c_next = (c + 1) % 16
    zh_prev = jnp.where(z_lo == 0, 1 - zh, zh)
    zh_next = jnp.where(z_lo == 3, 1 - zh, zh)

    def facet(half, place_x, which):
        return half * 8 + place_x * 2 + which

    def x_of(d):
        return (x + d) % 4

    f_core = facet(zh, x, 1 - core)
    f_z = facet(1 - zh, x, core)
    f_x = [f] + [facet(zh, x_of(d), core) for d in (1, 2, 3)]

    barrier = pltpu.get_barrier_semaphore()
    peers = [(f_core, c), (f_z, c), (f_x[1], c), (f_x[2], c), (f_x[3], c)]
    peers += [(facet(zh_prev, x_of(d), core), c_prev) for d in range(4)]
    peers += [(facet(zh_next, x_of(d), core), c_next) for d in range(4)]
    for peer in peers:
        pl.semaphore_signal(barrier, inc=1, device_id=peer, device_id_type=MESH)

    loads = [
        pltpu.make_async_copy(t_hbm, t_v, local_sem.at[2]),
        pltpu.make_async_copy(tt_hbm, tt_v, local_sem.at[3]),
        pltpu.make_async_copy(w_hbm, w_v.at[zh], local_sem.at[4]),
    ]
    spectra = [
        [
            pltpu.make_async_copy(
                x_hbm.at[col, part, pl.ds(256 * half, 256)],
                x_v.at[col, part, pl.ds(256 * half, 256)],
                local_sem.at[col],
            )
            for half in range(2) for part in range(2)
        ]
        for col in range(2)
    ]
    scalars = [
        pltpu.make_async_copy(source, target, local_sem.at[6 + index])
        for index, (source, target) in enumerate(
            ((offs_hbm, offs_ref), (colidx_hbm, colidx_ref), (sub_hbm, sub_ref))
        )
    ]
    for load in scalars:
        load.start()
    for load in spectra[0]:
        load.start()

    used = []

    def group():
        used.append(None)
        return rs.at[len(used) - 1]

    sent = []

    def send(src, dst, arrived, f_to, c_to=None):
        sent.append(math.prod(src.shape))
        pltpu.make_async_remote_copy(
            src_ref=src, dst_ref=dst, send_sem=ss.at[0], recv_sem=arrived,
            device_id=(f_to, c if c_to is None else c_to), device_id_type=MESH,
        ).start()

    def arrive(whole, arrived):
        pltpu.make_async_copy(whole, whole, arrived).wait()

    for load in scalars:
        load.wait()
    for load in spectra[1]:
        load.start()
    lane = iota((16, 128), 1)
    first, second = offs_ref[0, 0], offs_ref[0, 1]
    starts = []
    for col in range(2):
        starts.append(lax.shift_right_arithmetic(sub_ref[col], 2) - c * SHARD - HALF)

    def prepared(col):
        start = starts[col]
        column_pos = colidx_ref[col] * XA
        cosine, sine = phase(turns(column_pos, first, second, c * SHARD + start + iota((8, 128), 1)))
        cosine, sine = cosine[0:1], sine[0:1]
        spot = iota((8, 128), 1)
        spot = c * SHARD + jnp.where(spot < HALF, spot, SHARD - 128 + spot)
        cosine_e, sine_e = phase(turns(column_pos, first, second, spot))
        cosine_e, sine_e = cosine_e[0:1], sine_e[0:1]
        tile = jnp.clip(lax.shift_right_arithmetic(start, 7), 0, SHARD // 128 - 2)
        pick = (iota((256, 128), 0) + tile * 128 == iota((256, 128), 1) + start).astype(F32).astype(BF16)
        bits = [(jnp.full((128, 128), 0, I32) + tile) & (1 << bit) != 0 for bit in range(3)]
        return cosine, sine, cosine_e, sine_e, pick, bits

    wide = iota((128, 128), 1) < HALF

    def phased(col, cosine, sine, cosine_e, sine_e, pick, bits):
        for q in range(4):
            span = pl.ds(q * 128, 128)
            pairs = []
            for part in range(2):
                tiles = [x_v[col, part, span, 128 * i:128 * i + 128] for i in range(8)]
                for bit, width in ((2, 5), (1, 3), (0, 2)):
                    far = 1 << bit
                    tiles = [
                        jnp.where(bits[bit], tiles[i + far], tiles[i]) if i + far < len(tiles) else tiles[i]
                        for i in range(width)
                    ]
                pairs.append(jnp.concatenate(tiles, axis=1))
            main_re = dot(pairs[0], pick)
            main_im = dot(pairs[1], pick)
            out_re = (main_re * cosine + main_im * sine).astype(BF16)
            out_im = (main_im * cosine - main_re * sine).astype(BF16)
            edge_re = jnp.where(wide, x_v[col, 0, span, 0:128].astype(F32), x_v[col, 0, span, SHARD - 128:SHARD].astype(F32))
            edge_im = jnp.where(wide, x_v[col, 1, span, 0:128].astype(F32), x_v[col, 1, span, SHARD - 128:SHARD].astype(F32))
            e_re = edge_re * cosine_e + edge_im * sine_e
            e_im = edge_im * cosine_e - edge_re * sine_e
            swap_re = pltpu.roll(e_re, 64, 1)
            swap_im = pltpu.roll(e_im, 64, 1)
            for j in range(4):
                xx, cc = (q % 2) * 2 + j // 2, j % 2
                block = y.at[col, cc, xx, q // 2]
                a, b, d = 32 * j, 32 * j + 16, 32 * j + 32
                block[0:32] = out_re[a:d]
                block[32:64] = out_im[a:d]
                block[64:80] = jnp.where(lane < HALF, e_re[a:b], swap_re[b:d]).astype(BF16)
                block[80:96] = jnp.where(lane < HALF, e_im[a:b], swap_im[b:d]).astype(BF16)
                block[96:112] = jnp.where(lane < HALF, swap_re[a:b], e_re[b:d]).astype(BF16)
                block[112:128] = jnp.where(lane < HALF, swap_im[a:b], e_im[b:d]).astype(BF16)

    def total(*refs):
        result = refs[0][...].astype(F32)
        for ref in refs[1:]:
            result = result + ref[...].astype(F32)
        return result

    order = (2, 1, 3, 0)
    from_core = [group() for _ in range(2)]
    from_z_weights = group()
    ready = [prepared(col) for col in range(2)]
    row = iota((8, 128), 0)
    known = [starts[0], starts[1]] + [(colidx_ref[col] * XA * first) & 65535 for col in range(2)] + [second]
    facts = jnp.zeros((8, 128), I32)
    for index, value in enumerate(known):
        facts = jnp.where(row == index, value, facts)
    info[...] = facts.astype(F32)
    for col in range(2):
        arrive(x_v.at[col], local_sem.at[col])
        if col == 1:
            for load in loads:
                load.start()
        phased(col, *ready[col])
        if col == 0:
            pl.semaphore_wait(barrier, len(peers))
        send(y.at[col, 1 - core], r1.at[col], from_core[col], f_core)
    send(w_hbm, w_v.at[zh], from_z_weights, f_z)

    from_x = [group() for _ in range(2)]
    from_near = [group() for _ in range(2)]
    for col in range(2):
        arrive(r1.at[col], from_core[col])
        for d in order:
            xx = x_of(d)
            y[col, core, xx] = total(y.at[col, core, xx], r1.at[col, xx]).astype(BF16)
            block = y.at[col, core, xx]
            send(block.at[:, pl.ds(64, 32)], ex.at[col, 1, d], from_near[col], facet(zh_prev, xx, core), c_prev)
            send(block.at[:, pl.ds(96, 32)], ex.at[col, 0, d], from_near[col], facet(zh_next, xx, core), c_next)
            if d:
                send(block.at[:, pl.ds(0, 64)], rx.at[col, d - 1], from_x[col], f_x[d])

    def matrix(source, window, start):
        cell = (source & 63) + jnp.where(source < 128, -HALF, SHARD) - start
        same = (lax.shift_right_logical(source, 6) & 1) == lax.shift_right_logical(window, 7)
        return jnp.where(same & (cell == (window & 127)), 1.0, 0.0).astype(BF16)

    side0, side1 = iota((256, 256), 0), iota((256, 256), 1)
    gather_in = [matrix(side0, side1, start) for start in starts]
    gather_out = [matrix(side1, side0, start) for start in starts]

    from_z = [group() for _ in range(2)]
    for col in range(2):
        arrive(rx.at[col], from_x[col])
        main = total(y.at[col, core, x, :, pl.ds(0, 64)], rx.at[col, 0], rx.at[col, 1], rx.at[col, 2])
        arrive(ex.at[col], from_near[col])
        low, high = (total(*(ex.at[col, side, d] for d in range(4))).reshape(64, 128) for side in range(2))
        edge = dot(jnp.concatenate([low, high], axis=1).astype(BF16), gather_in[col])
        for half in range(2):
            for part in range(2):
                a = half * 32 + part * 16
                reach = jnp.concatenate([edge[a:a + 16, 0:128], edge[a:a + 16, 128:256]], axis=0)
                rows = slice(part * 32, part * 32 + 32)
                s2[col, half, rows] = (main[half, rows] + reach).astype(BF16)
        send(s2.at[col], rz.at[col], from_z[col], f_z)

    for load in loads:
        load.wait()
    arrive(w_v.at[1 - zh], from_z_weights)

    from_mains = [[group() for _ in range(3)] for _ in range(2)]
    from_edges = [[group() for _ in range(4)] for _ in range(2)]
    passed = [[group() for _ in range(2)] for _ in range(2)]
    for col in range(2):
        arrive(rz.at[col], from_z[col])
        main = total(s2.at[col], rz.at[col])
        window = jnp.concatenate(
            [main[half, part * 32:part * 32 + 32] for part in range(2) for half in range(2)], axis=0
        ).astype(BF16)
        prod = dot(window, t_v[...])
        cells_re = (prod[0:64, 0:XM] - prod[64:128, XM:2 * XM]).astype(BF16)
        cells_im = (prod[0:64, XM:2 * XM] + prod[64:128, 0:XM]).astype(BF16)
        weight = jnp.concatenate([w_v[0, col], w_v[1, col]], axis=0).astype(F32)
        scaled_re = (cells_re.astype(F32) * weight).astype(BF16)
        scaled_im = (cells_im.astype(F32) * weight).astype(BF16)
        prod = dot(jnp.concatenate([scaled_re, scaled_im], axis=0), tt_v[...])
        back_re = (prod[0:64, 0:WM] + prod[64:128, WM:2 * WM]).astype(BF16)
        back_im = (prod[64:128, 0:WM] - prod[0:64, WM:2 * WM]).astype(BF16)
        packed = []
        for half in range(2):
            block = g.at[col, half, x, core]
            a = half * 32
            block[0:32] = back_re[a:a + 32]
            block[32:64] = back_im[a:a + 32]
            for back in (back_re, back_im):
                packed.append(jnp.concatenate([back[a:a + 16], back[a + 16:a + 32]], axis=1))
        home = g.at[col, :, x, core, pl.ds(0, 64)]
        for d in (2, 1, 3):
            send(home, home, from_mains[col][d - 1], f_x[d])
        send(home, home, passed[col][0], f_core)
        out_edge = dot(jnp.concatenate(packed, axis=0), gather_out[col]).astype(BF16)
        eo[col, 0] = out_edge[:, 0:128].reshape(2, 32, 128)
        eo[col, 1] = out_edge[:, 128:256].reshape(2, 32, 128)
        low, high = g.at[col, :, x, core, pl.ds(64, 32)], g.at[col, :, x, core, pl.ds(96, 32)]
        for d in order:
            send(eo.at[col, 0], high, from_edges[col][d], facet(zh_prev, x_of(d), core), c_prev)
            send(eo.at[col, 1], low, from_edges[col][d], facet(zh_next, x_of(d), core), c_next)
        for half in range(2):
            grid_v[half, col, 0] = cells_re[half * 32:half * 32 + 32]
            grid_v[half, col, 1] = cells_im[half * 32:half * 32 + 32]

    for col in range(2):
        for d, rows in ((1, 0), (3, 0), (2, 64), (1, 64), (3, 64), (0, 64), (2, 0)):
            block = g.at[col, :, x_of(4 - d), core, pl.ds(rows, 64)]
            arrive(block, from_edges[col][d] if rows else from_mains[col][d - 1])
            send(block, block, passed[col][1 if rows else 0], f_core)

    grid_copy = pltpu.make_async_copy(grid_v.at[zh], grid_out, local_sem.at[5])
    grid_copy.start()
    for col in range(2):
        for half in range(2):
            arrive(g.at[col, :, :, 1 - core, pl.ds(64 * half, 64)], passed[col][half])

    assert len(used) == N_GROUPS
    every = sum(sent) // SHARD
    arrive(x_v.reshape(2 * 2 * XM, SHARD).at[pl.ds(0, every)], ss.at[0])
    grid_copy.wait()


N_GROUPS = 27


def exchange(offsets, column_index, subgrid_offsets, spectra, weights):
    table, table_t = tables()
    hbm = pl.BlockSpec(memory_space=pltpu.HBM)
    vmem = pl.BlockSpec(memory_space=pltpu.VMEM)
    return pl.pallas_call(
        exchange_kernel,
        out_shape=(
            pltpu.VMEM((2, 2, 32, XM), BF16),
            pltpu.VMEM((2, 2, 4, 2, 128, 128), BF16),
            pltpu.VMEM((8, 128), F32),
        ),
        in_specs=[hbm] * 7,
        out_specs=(vmem, vmem, vmem),
        scratch_shapes=[
            pltpu.SMEM((1, 2), I32),
            pltpu.SMEM((2,), I32),
            pltpu.SMEM((2,), I32),
            pltpu.VMEM((2, 2, XM, SHARD), BF16),
            pltpu.VMEM((2, 2, 32, XM), BF16),
            pltpu.VMEM((WM, 2 * XM), BF16),
            pltpu.VMEM((XM, 2 * WM), BF16),
            pltpu.VMEM((2, 2, 4, 2, 128, 128), BF16),
            pltpu.VMEM((2, 4, 2, 128, 128), BF16),
            pltpu.VMEM((2, 3, 2, 64, 128), BF16),
            pltpu.VMEM((2, 2, 4, 2, 32, 128), BF16),
            pltpu.VMEM((2, 2, 64, 128), BF16),
            pltpu.VMEM((2, 2, 64, 128), BF16),
            pltpu.VMEM((2, 2, 2, 32, 128), BF16),
            pltpu.VMEM((2, 2, 2, 32, XM), BF16),
            pltpu.SemaphoreType.DMA((9,)),
            pltpu.SemaphoreType.DMA((1,)),
            pltpu.SemaphoreType.DMA((N_GROUPS,)),
        ],
        compiler_params=pltpu.CompilerParams(collective_id=0, has_side_effects=True),
        name="exchange",
    )(offsets, column_index, subgrid_offsets, spectra, weights, jnp.asarray(table), jnp.asarray(table_t))


def place_kernel(u_ref, grid_ref, info_ref, out_hbm, grid_hbm, out, sem):
    grid_copy = pltpu.make_async_copy(grid_ref, grid_hbm, sem.at[0])
    grid_copy.start()
    known = [jnp.max(info_ref[index:index + 1, :]).astype(I32) for index in range(5)]
    c = lax.axis_index("col")
    second = known[4]
    spot = iota((8, 128), 1)
    spot = c * SHARD + jnp.where(spot < HALF, spot, SHARD - 128 + spot)
    lane = iota((16, 128), 1)
    wide = iota((32, 128), 1) < HALF
    for col in range(2):
        start = known[col]
        base = jnp.clip(lax.shift_right_arithmetic(start, 7), 0, SHARD // 128 - 2) * 128
        cosine, sine = phase(turns(known[2 + col], 1, second, c * SHARD + base + iota((8, 256), 1)))
        cosine, sine = cosine[0:1], sine[0:1]
        cosine_e, sine_e = phase(turns(known[2 + col], 1, second, spot))
        cosine_e, sine_e = cosine_e[0:1], sine_e[0:1]
        put = (iota((128, 256), 1) + base == iota((128, 256), 0) + start).astype(F32).astype(BF16)
        tiles = pl.ds(pl.multiple_of(base, 128), 256)

        for q in range(4):
            span = pl.ds(q * 128, 128)
            out[col, :, span] = jnp.zeros((2, 128, SHARD), BF16)
            some = u_ref.at[col, q // 2, pl.ds((q % 2) * 2, 2)]
            moved = dot(some[:, :, 0:64].reshape(256, 128), put)
            for j in range(4):
                block = some.at[j // 2, j % 2]
                rows = pl.ds(q * 128 + 32 * j, 32)
                low_re, low_im = block[64:80].astype(F32), block[80:96].astype(F32)
                top_re, top_im = block[96:112].astype(F32), block[112:128].astype(F32)
                edges = []
                for low, top in ((low_re, top_re), (low_im, top_im)):
                    edges.append(jnp.concatenate([
                        jnp.where(lane < HALF, low, pltpu.roll(top, 64, 1)),
                        jnp.where(lane < HALF, pltpu.roll(low, 64, 1), top),
                    ], axis=0))
                edge_re = edges[0] * cosine_e - edges[1] * sine_e
                edge_im = edges[1] * cosine_e + edges[0] * sine_e
                zero = jnp.zeros_like(edge_re)
                for part, edge in ((0, edge_re), (1, edge_im)):
                    out[col, part, rows, 0:128] = jnp.where(wide, edge, zero).astype(BF16)
                    out[col, part, rows, SHARD - 128:SHARD] = jnp.where(wide, zero, edge).astype(BF16)
                main_re, main_im = moved[64 * j:64 * j + 32], moved[64 * j + 32:64 * j + 64]
                out_re = main_re * cosine - main_im * sine
                out_im = main_im * cosine + main_re * sine
                for part, value in ((0, out_re), (1, out_im)):
                    out[col, part, rows, tiles] = (out[col, part, rows, tiles].astype(F32) + value).astype(BF16)
            pltpu.make_async_copy(out.at[col, :, span], out_hbm.at[col, :, span], sem.at[1 + col * 4 + q]).start()

    for col in range(2):
        for q in range(4):
            span = pl.ds(q * 128, 128)
            pltpu.make_async_copy(out.at[col, :, span], out_hbm.at[col, :, span], sem.at[1 + col * 4 + q]).wait()
    grid_copy.wait()


def place(gathered, grids, info):
    hbm = pl.BlockSpec(memory_space=pltpu.HBM)
    vmem = pl.BlockSpec(memory_space=pltpu.VMEM)
    gathered = pltpu.with_memory_space_constraint(gathered, pltpu.VMEM)
    grids = pltpu.with_memory_space_constraint(grids, pltpu.VMEM)
    info = pltpu.with_memory_space_constraint(info, pltpu.VMEM)
    return pl.pallas_call(
        place_kernel,
        out_shape=(
            jax.ShapeDtypeStruct((2, 2, XM, SHARD), BF16),
            jax.ShapeDtypeStruct((2, 2, 32, XM), BF16),
        ),
        in_specs=[vmem, vmem, vmem],
        out_specs=(hbm, hbm),
        scratch_shapes=[
            pltpu.VMEM((2, 2, XM, SHARD), BF16),
            pltpu.SemaphoreType.DMA((9,)),
        ],
        compiler_params=pltpu.CompilerParams(vmem_limit_bytes=16 << 20),
        name="place",
    )(gathered, grids, info)


def per_device(facet_spectra, facet_offsets, column_index, subgrid_offsets, weights):
    spectra = facet_spectra.reshape(2, 2, XM, SHARD)
    subgrid_offsets = subgrid_offsets.reshape(2)
    grids, gathered, info = exchange(
        facet_offsets, column_index, subgrid_offsets, spectra, weights.reshape(2, 32, XM)
    )
    updates, grids = place(gathered, grids, info)
    return grids.reshape(2, 1, 2, 32, XM), updates.reshape(2, 1, 2, XM, SHARD)


def solution(mesh):
    in_specs = (
        P(None, "facet", None, None, "col"),
        P("facet", None),
        P(),
        P(None, "col"),
        P(None, "col", "facet", None),
    )
    out_specs = (P(None, "col", None, "facet", None), P(None, "facet", None, None, "col"))
    return jax.shard_map(
        per_device, mesh=mesh, in_specs=in_specs, out_specs=out_specs, check_vma=False
    )
```
